256 devices in a mesh: dp: 32 (over z, y_hi, core), fsdp: 8 (over y_lo, x).
Axes of the slice: x: 4, y: 4 (y_hi: 2, y_lo: 2; y = y_hi * 2 + y_lo), z: 8, core: 2. Of those that a mesh axis runs over, the one named last changes fastest.
Arguments:
- hidden: bfloat16 [131072, 1152], P(('dp', 'fsdp')), may hold values from -6 to 6
- text_ids: int32 [8192, 16], P(('dp', 'fsdp')), may hold values from 0 to 31999, as said below
- ln_gain: float32 [1152], replicated, may hold values from 0.5 to 1.5
- ln_bias: float32 [1152], replicated, may hold values from -2 to 2
- fc1_weight: bfloat16 [1152, 4304], P(None, 'fsdp'), may hold values from -0.1875 to 0.1875
- fc1_bias: float32 [4304], replicated, may hold values from -3 to 3
- fc2_weight: bfloat16 [4304, 1152], P('fsdp'), may hold values from -0.09375 to 0.09375
- fc2_bias: float32 [1152], replicated, may hold values from -3 to 3
- final_gain: float32 [1152], replicated, may hold values from 0.5 to 1.5
- final_bias: float32 [1152], replicated, may hold values from -0.2 to 0.2
- head_weight: bfloat16 [1152, 1152], replicated, may hold values from -0.1875 to 0.1875
- head_bias: float32 [1152], replicated, may hold values from -0.3 to 0.3
- image_emb: bfloat16 [8192, 1152], P(('dp', 'fsdp')), may hold values from -6 to 6
- teacher_logits: bfloat16 [8192, 12, 256], P('dp', None, 'fsdp'), may hold values from -12 to 12
- logit_scale: float32 [1], replicated, may hold values from 4 to 16
- logit_bias: float32 [1], replicated, may hold values from -3 to 0
Outputs:
- image_grad: float32 [8192, 1152], P(('dp', 'fsdp'))
The draws below stay inside these ranges and needn't reach their ends.
Inputs may be any that keep to these rules, and one draw needn't show every extreme that they name: `text_ids`: 0 marks padding after a text's end; every text has at least one token and the tokens of a text come first.
All inputs are finite; a program needn't handle non-finite values.
Results may differ from the reference program's by a relative error of at most 0.0018.
Values may be sent and summed in bfloat16 or wider, within the bound.
No kernel may reach another device: no remote copies, remote signals or barrier semaphores. Data moves between devices by JAX's collectives and lax.ppermute only.
A program may use at most 128 MiB of HBM per device.

```python
import math
import jax
import jax.numpy as jnp
from jax import lax

D = 1152
FF = 4304
VOCAB = 32000
SEQ = 16
WINDOW = 12
PAIRS_DEV = 32
GROUP = 256
TEXTS = 8192
TOKENS = 131072
N_DP = 32


def draw_text_ids(key, part):
    key_len, key_ids = jax.random.split(jax.random.fold_in(key, 7))
    lengths = jax.random.randint(key_len, (TEXTS, 1), 1, SEQ + 1)
    lengths = lengths.at[0, 0].set(1)
    tokens = jax.random.randint(key_ids, (TEXTS, SEQ), 1, VOCAB)
    tokens = tokens.at[0, 0].set(VOCAB - 1)
    place = jnp.arange(SEQ)[None, :]
    return jnp.where(place < lengths, tokens, 0).astype(jnp.int32)


def steps_of(stream_key, shape, cuts, low, largest):
    loudness = 1.0
    for dim, parts in cuts:
        steps = jax.random.uniform(jax.random.fold_in(jax.random.fold_in(stream_key, 6), dim), (parts,), jnp.float32, low / len(cuts), largest / len(cuts))
        loudness = loudness * jnp.repeat(jnp.exp(steps), shape[dim] // parts).reshape((-1,) + (1,) * (len(shape) - 1 - dim))
    return loudness


def normal_values(rng, shape, scale, reach, cuts=(), kind=jnp.bfloat16):
    drawn = scale * jax.random.normal(rng, shape, jnp.float32)
    if cuts:
        drawn = drawn * steps_of(rng, shape, cuts, -0.22, 0.18)
    return jnp.clip(drawn, -reach, reach).astype(kind)


def setup_inputs(seed: int = 0) -> dict:
    arg_keys = jax.random.split(jax.random.key(seed), 17)
    return {
        "hidden": normal_values(arg_keys[0], (TOKENS, D), 1.0, 6.0, ((0, 256),)),
        "text_ids": draw_text_ids(jax.random.fold_in(arg_keys[16], 71), 0),
        "ln_gain": jnp.clip(1.0 + 0.1 * jax.random.normal(arg_keys[2], (D,), jnp.float32), 0.5, 1.5),
        "ln_bias": normal_values(arg_keys[3], (D,), 0.3, 2.0, (), jnp.float32),
        "fc1_weight": normal_values(arg_keys[4], (D, FF), D ** -0.5, 0.1875, ((1, 8),)),
        "fc1_bias": normal_values(arg_keys[5], (FF,), 0.5, 3.0, (), jnp.float32),
        "fc2_weight": normal_values(arg_keys[6], (FF, D), FF ** -0.5, 0.09375, ((0, 8),)),
        "fc2_bias": normal_values(arg_keys[7], (D,), 0.5, 3.0, (), jnp.float32),
        "final_gain": jnp.clip(1.0 + 0.1 * jax.random.normal(arg_keys[8], (D,), jnp.float32), 0.5, 1.5),
        "final_bias": normal_values(arg_keys[9], (D,), 0.03, 0.2, (), jnp.float32),
        "head_weight": normal_values(arg_keys[10], (D, D), D ** -0.5, 0.1875),
        "head_bias": normal_values(arg_keys[11], (D,), 0.05, 0.3, (), jnp.float32),
        "image_emb": normal_values(arg_keys[12], (TEXTS, D), 1.0, 6.0, ((0, 256),)),
        "teacher_logits": normal_values(arg_keys[13], (TEXTS, WINDOW, GROUP), 3.0, 12.0, ((0, 32), (2, 8))),
        "logit_scale": jnp.clip(jnp.exp(jax.random.uniform(arg_keys[14], (1,), jnp.float32, math.log(4.0), math.log(16.0))), 4.0, 16.0),
        "logit_bias": jnp.clip(jax.random.uniform(arg_keys[15], (1,), jnp.float32, -3.0, 0.0), -3.0, 0.0),
    }


def layer_norm(values, gain, shift):
    centre = lax.optimization_barrier(jnp.mean(values, axis=-1, keepdims=True))
    spread = lax.optimization_barrier(jnp.mean((values - centre) ** 2, axis=-1, keepdims=True))
    return (values - centre) * lax.rsqrt(spread + 1e-06) * gain + shift

def reference(hidden, text_ids, ln_gain, ln_bias, fc1_weight, fc1_bias, fc2_weight, fc2_bias, final_gain, final_bias, head_weight, head_bias, image_emb, teacher_logits, logit_scale, logit_bias):
    blocks = hidden.reshape(-1, PAIRS_DEV * SEQ, D)
    id_blocks = text_ids.reshape(-1, PAIRS_DEV, SEQ)

    def encode(pair):
        tokens, ids = pair
        flat = tokens.astype(jnp.float32)
        normed = layer_norm(flat, ln_gain, ln_bias).astype(jnp.bfloat16)
        pre = jnp.dot(normed, fc1_weight, preferred_element_type=jnp.float32) + fc1_bias
        act = jax.nn.gelu(pre, approximate=True).astype(jnp.bfloat16)
        out = flat + jnp.dot(act, fc2_weight, preferred_element_type=jnp.float32) + fc2_bias
        final = layer_norm(out, final_gain, final_bias).reshape(PAIRS_DEV, SEQ, D)
        keep = (ids != 0).astype(jnp.float32)
        pooled = lax.optimization_barrier(jnp.sum(final * keep[:, :, None], axis=1)) / lax.optimization_barrier(jnp.sum(keep, axis=1))[:, None]
        emb = jnp.dot(pooled.astype(jnp.bfloat16), head_weight, preferred_element_type=jnp.float32) + head_bias
        return (emb * lax.rsqrt(lax.optimization_barrier(jnp.sum(emb * emb, axis=-1, keepdims=True)) + 1e-06)).astype(jnp.bfloat16)
    units = lax.map(encode, (blocks, id_blocks)).reshape(N_DP, -1, D)
    images = image_emb.astype(jnp.float32)
    image_unit = (images * lax.rsqrt(lax.optimization_barrier(jnp.sum(images * images, axis=-1, keepdims=True)) + 1e-06)).astype(jnp.bfloat16)
    image_unit = image_unit.reshape(N_DP, -1, D).astype(jnp.float32)
    teach = teacher_logits.reshape(N_DP, -1, WINDOW, teacher_logits.shape[2])
    scale = logit_scale[0]
    offset = logit_bias[0]
    total = jnp.zeros(image_unit.shape, jnp.float32)
    for step in range(WINDOW):
        texts = jnp.roll(units, step, axis=0).astype(jnp.float32)
        target = jax.nn.sigmoid(jnp.roll(teach[:, :, step, :], step, axis=0).astype(jnp.float32))
        score = scale * jnp.einsum('kgd,kjd->kgj', texts, image_unit) + offset
        weight = (jax.nn.sigmoid(score) - target).astype(jnp.bfloat16).astype(jnp.float32)
        total = total + jnp.einsum('kgj,kgd->kjd', weight, texts)
    return (scale * total).reshape(-1, D)
```

```python
import functools

import jax
import jax.numpy as jnp
from jax import lax
from jax.experimental import pallas as pl
from jax.experimental.pallas import tpu as pltpu
from jax.sharding import PartitionSpec as P

AXES = ("dp", "fsdp")
DEVICES = 256
HALF = 272


def place_of(device):
    dp, fs = divmod(device, 8)
    return fs % 4, ((dp >> 1) & 1) * 2 + (fs >> 2), dp >> 2, dp & 1


def device_at(x, y, z, c):
    x, y, z = x % 4, y % 4, z % 8
    return (z * 4 + (y >> 1) * 2 + c) * 8 + (y & 1) * 4 + x


def come_from(array, dx=0, dy=0, dz=0, dc=0):
    pairs = []
    for target in range(DEVICES):
        x, y, z, c = place_of(target)
        pairs.append((device_at(x + dx, y + dy, z + dz, c ^ dc), target))
    return lax.ppermute(array, AXES, pairs)


def here():
    dp, fs = lax.axis_index("dp"), lax.axis_index("fsdp")
    return fs % 4, ((dp // 2) % 2) * 2 + fs // 4, dp // 4, dp % 2


def normalise(values, gain, shift):
    centre = jnp.mean(values, axis=-1, keepdims=True)
    spread = jnp.mean((values - centre) ** 2, axis=-1, keepdims=True)
    return (values - centre) * lax.rsqrt(spread + 1e-06) * gain + shift


def mlp_term(normed, up, bias, down):
    pre = (
        lax.dot_general(normed, up, (((1,), (1,)), ((), ())), preferred_element_type=jnp.float32)
        + bias
    )
    act = jax.nn.gelu(pre, approximate=True).astype(jnp.bfloat16)
    return jnp.dot(act, down, preferred_element_type=jnp.float32)


def first_kernel(hidden, gain, shift, up, bias, down, normed, total):
    flat = hidden[...].astype(jnp.float32)
    normed[...] = normalise(flat, gain[...], shift[...]).astype(jnp.bfloat16)
    total[...] = mlp_term(normed[...], up[...], bias[...], down[...])


def fetch_pieces(count, mine, other, up, down, sems):
    core = here()[3]

    def copies(k, first, second):
        rows = pl.ds(k * HALF, HALF)
        return (
            pltpu.make_async_copy(first, up.at[rows], sems.at[k, 0]),
            pltpu.make_async_copy(second, down.at[rows], sems.at[k, 1]),
        )

    @pl.when(core == 0)
    def _():
        for k in range(count):
            for copy in copies(k, mine[k], other[k]):
                copy.start()

    @pl.when(core == 1)
    def _():
        for k in range(count):
            for copy in copies(k, other[k], mine[k]):
                copy.start()

    for k in range(count):
        for copy in copies(k, mine[k], other[k]):
            copy.wait()


def middle_kernel(count, *refs):
    normed, before, bias = refs[:3]
    mine, other = refs[3 : 3 + count], refs[3 + count : 3 + 2 * count]
    total, up, down, sems = refs[3 + 2 * count :]
    fetch_pieces(count, mine, other, up, down, sems)
    total[...] = before[...] + mlp_term(normed[...], up[...], bias[...], down[...])


def last_kernel(count, *refs):
    normed, before, bias, hidden, fc2_bias, gain, shift, keep, head, head_bias = refs[:10]
    mine, other = refs[10 : 10 + count], refs[10 + count : 10 + 2 * count]
    unit, up, down, sems = refs[10 + 2 * count :]
    fetch_pieces(count, mine, other, up, down, sems)
    mixed = before[...] + mlp_term(normed[...], up[...], bias[...], down[...])
    out = hidden[...].astype(jnp.float32) + mixed + fc2_bias[...]
    final = normalise(out, gain[...], shift[...])
    texts, width = unit.shape
    seq = out.shape[0] // texts
    kept = keep[...]
    summed = jnp.sum((final * kept).reshape(texts, seq, width), axis=1)
    number = jnp.sum(jnp.broadcast_to(kept, (texts * seq, 128)).reshape(texts, seq, 128), axis=1)
    pooled = (summed / number[:, :1]).astype(jnp.bfloat16)
    emb = jnp.dot(pooled, head[...], preferred_element_type=jnp.float32) + head_bias[...]
    unit[...] = (emb * lax.rsqrt(jnp.sum(emb * emb, axis=-1, keepdims=True) + 1e-06)).astype(
        jnp.bfloat16
    )


NEAR = (0, 1, -1, 2)
ROWS = tuple((dy, dc) for dc in (0, 1) for dy in NEAR)


def score_kernel(scalars, *refs):
    rows, images, tiles = refs[:8], refs[8:12], refs[12:16]
    grads, texts, pictures, sems = refs[16:20], refs[20], refs[21], refs[22]
    x, y, _, c = here()
    column = (y // 2) * 2 + c
    size, width = images[0].shape
    copies = []
    for r, (dy, dc) in enumerate(ROWS):
        there_y = (y + dy + 4) % 4
        there_c = (c + dc) % 2
        block = (there_y // 2) * 2 + there_c
        for e, dx in enumerate(NEAR):
            slot = block * 8 + (there_y % 2) * 4 + (x + dx + 4) % 4
            start = pl.multiple_of(slot * size, size)
            copy = pltpu.make_async_copy(
                rows[r].at[pl.ds(e * size, size)], texts.at[pl.ds(start, size)], sems.at[r, e]
            )
            copy.start()
            copies.append(copy)
    for d in range(4):
        pictures[pl.ds(d * size, size)] = images[d][...]
    for copy in copies:
        copy.wait()
    scale, offset = scalars[0], scalars[1]
    pics = pictures[...]
    group = 8 * size
    total = jnp.zeros((4 * size, width), jnp.float32)
    far = lax.broadcasted_iota(jnp.int32, (4 * size, group), 0) // size
    for m in range(4):
        block = (column // 2 + m // 2) % 2 * 2 + (column % 2 + m % 2) % 2
        units = texts[pl.ds(pl.multiple_of(block * group, group), group)]
        score = (
            scale
            * lax.dot_general(
                pics, units, (((1,), (1,)), ((), ())), preferred_element_type=jnp.float32
            )
            + offset
        )
        target = tiles[m][...].reshape(4 * size, group).astype(jnp.float32)
        step = 4 * far + (column - block)
        weight = jnp.where(
            (step >= 0) & (step < 12), jax.nn.sigmoid(score) - jax.nn.sigmoid(target), 0.0
        ).astype(jnp.bfloat16)
        total = total + jnp.dot(weight, units, preferred_element_type=jnp.float32)
    for d in range(4):
        grads[d][...] = total[d * size : (d + 1) * size].astype(grads[d].dtype)


VMEM = pl.BlockSpec(memory_space=pltpu.VMEM)
ANY = pl.BlockSpec(memory_space=pl.ANY)
SMEM = pl.BlockSpec(memory_space=pltpu.SMEM)


def mlp_scratch(count, width):
    return [
        pltpu.VMEM((count * HALF, width), jnp.bfloat16),
        pltpu.VMEM((count * HALF, width), jnp.bfloat16),
        pltpu.SemaphoreType.DMA((count, 2)),
    ]


def row(vector):
    return vector.reshape(1, -1)


def on_device(
    hidden,
    text_ids,
    ln_gain,
    ln_bias,
    fc1_weight,
    fc1_bias,
    fc2_weight,
    fc2_bias,
    final_gain,
    final_bias,
    head_weight,
    head_bias,
    image_emb,
    teacher_logits,
    logit_scale,
    logit_bias,
):
    tokens, width = hidden.shape
    texts_here, _ = text_ids.shape
    window = teacher_logits.shape[1]
    hidden_here = fc1_weight.shape[1]
    x, y, z, c = here()
    odd = z % 2

    up, down = fc1_weight.T, fc2_weight
    own = jnp.pad(jnp.where(c == 0, up, down), ((0, 2 * HALF - hidden_here), (0, 0)))
    own_p = lax.dynamic_slice_in_dim(own, odd * HALF, HALF, 0)
    own_q = lax.dynamic_slice_in_dim(own, (1 - odd) * HALF, HALF, 0)

    right_p = come_from(own_p, dx=1)
    left_p = come_from(own_p, dx=-1)
    flip_p = come_from(own_p, dy=1)
    flip_q = come_from(own_q, dy=-1)
    right_q = come_from(right_p, dz=1)
    left_q = come_from(left_p, dz=-1)
    flip_right_p = come_from(right_p, dy=1)
    flip_left_p = come_from(left_p, dy=-1)
    over_p = come_from(right_p, dx=1)
    flip_left_q = come_from(flip_q, dx=-1)
    flip_right_q = come_from(flip_right_p, dz=1)
    over_q = come_from(over_p, dz=-1)
    flip_over_p = come_from(over_p, dy=1)
    flip_over_q = come_from(flip_left_q, dx=-1)
    waves = (
        ((right_p, 1, 0, 0), (left_p, -1, 0, 0), (flip_p, 0, 1, 0), (flip_q, 0, 1, 1)),
        (
            (right_q, 1, 0, 1),
            (left_q, -1, 0, 1),
            (flip_right_p, 1, 1, 0),
            (flip_left_p, -1, 1, 0),
            (over_p, 2, 0, 0),
            (flip_left_q, -1, 1, 1),
        ),
        (
            (flip_right_q, 1, 1, 1),
            (over_q, 2, 0, 1),
            (flip_over_p, 2, 1, 0),
            (flip_over_q, 2, 1, 1),
        ),
    )

    shards = fc1_bias.shape[0] // hidden_here
    biases = fc1_bias.reshape(shards, hidden_here)
    own_bias = lax.dynamic_slice_in_dim(biases, (y % 2) * 4 + x, 1, 0)
    halves = jnp.pad(biases, ((0, 0), (0, 2 * HALF - hidden_here))).reshape(2 * shards, HALF)

    def bias_of(wave):
        places = [
            (((y + dy) % 2) * 4 + (x + dx + 4) % 4) * 2 + (odd + other) % 2
            for _, dx, dy, other in wave
        ]
        return jnp.concatenate(
            [lax.dynamic_slice_in_dim(halves, p, 1, 0) for p in places], axis=1
        )

    normed, total = pl.pallas_call(
        first_kernel,
        out_shape=(
            jax.ShapeDtypeStruct((tokens, width), jnp.bfloat16),
            jax.ShapeDtypeStruct((tokens, width), jnp.float32),
        ),
        in_specs=[VMEM] * 6,
        out_specs=(VMEM, VMEM),
        name="mlp_first",
    )(hidden, row(ln_gain), row(ln_bias), up, own_bias, down)

    for wave in waves[:2]:
        count = len(wave)
        mine = [piece for piece, *_ in wave]
        other = [come_from(piece, dc=1) for piece in mine]
        total = pl.pallas_call(
            functools.partial(middle_kernel, count),
            out_shape=jax.ShapeDtypeStruct((tokens, width), jnp.float32),
            in_specs=[VMEM] * 3 + [ANY] * (2 * count),
            out_specs=VMEM,
            scratch_shapes=mlp_scratch(count, width),
            name=f"mlp_middle_{count}",
        )(normed, total, bias_of(wave), *mine, *other)

    keep = (text_ids != 0).astype(jnp.float32).reshape(tokens, 1)
    wave = waves[2]
    count = len(wave)
    mine = [piece for piece, *_ in wave]
    other = [come_from(piece, dc=1) for piece in mine]
    text_unit = pl.pallas_call(
        functools.partial(last_kernel, count),
        out_shape=jax.ShapeDtypeStruct((texts_here, width), jnp.bfloat16),
        in_specs=[VMEM] * 10 + [ANY] * (2 * count),
        out_specs=VMEM,
        scratch_shapes=mlp_scratch(count, width),
        name="mlp_last",
    )(
        normed,
        total,
        bias_of(wave),
        hidden,
        row(fc2_bias),
        row(final_gain),
        row(final_bias),
        keep,
        head_weight,
        row(head_bias),
        *mine,
        *other,
    )

    images = image_emb.astype(jnp.float32)
    image_unit = (
        images * lax.rsqrt(jnp.sum(images * images, axis=-1, keepdims=True) + 1e-06)
    ).astype(jnp.bfloat16)
    pictures = [image_unit] + [come_from(image_unit, dz=d) for d in (1, 2, 3)]
    column = (y // 2) * 2 + c
    tiles = jnp.pad(jnp.transpose(teacher_logits, (1, 2, 0)), ((3, 4), (0, 0), (0, 0)))
    tile_sets = []
    for m in range(4):
        target = (column // 2 + m // 2) % 2 * 2 + (column % 2 + m % 2) % 2
        part = lax.dynamic_slice_in_dim(tiles, 3 + target - column, 13, 0)[::4]
        tile_sets.append(come_from(part, dy=2 * (m // 2), dc=m % 2) if m else part)

    near_x = [text_unit] + [come_from(text_unit, dx=d) for d in NEAR[1:]]
    line = jnp.concatenate(near_x, axis=0)
    lines = [line] + [come_from(line, dy=d) for d in NEAR[1:]]
    lines = lines + [come_from(part, dc=1) for part in lines]
    scalars = jnp.concatenate([logit_scale, logit_bias])
    grads = pl.pallas_call(
        score_kernel,
        out_shape=tuple(
            jax.ShapeDtypeStruct((texts_here, width), kind)
            for kind in (jnp.float32, jnp.bfloat16, jnp.bfloat16, jnp.bfloat16)
        ),
        in_specs=[SMEM] + [ANY] * 8 + [VMEM] * 8,
        out_specs=(VMEM,) * 4,
        scratch_shapes=[
            pltpu.VMEM((4 * 8 * texts_here, width), jnp.bfloat16),
            pltpu.VMEM((4 * texts_here, width), jnp.bfloat16),
            pltpu.SemaphoreType.DMA((8, 4)),
        ],
        name="scores",
    )(scalars, *lines, *pictures, *tile_sets)
    total = grads[0]
    for d in (1, 2, 3):
        total = total + come_from(grads[d], dz=-d).astype(jnp.float32)
    return logit_scale[0] * total


def solution(mesh):
    placed = (
        P(("dp", "fsdp"), None),
        P(("dp", "fsdp"), None),
        P(),
        P(),
        P(None, "fsdp"),
        P(),
        P("fsdp", None),
        P(),
        P(),
        P(),
        P(),
        P(),
        P(("dp", "fsdp"), None),
        P("dp", None, "fsdp"),
        P(),
        P(),
    )
    return jax.shard_map(
        on_device, mesh=mesh, in_specs=placed, out_specs=P(("dp", "fsdp"), None), check_vma=False
    )
```

```python
import functools

import jax
import jax.numpy as jnp
from jax import lax
from jax.experimental import pallas as pl
from jax.experimental.pallas import tpu as pltpu
from jax.sharding import PartitionSpec as P

AXES = ("dp", "fsdp")
DEVICES = 256
HALF = 272


def place_of(device):
    dp, fs = divmod(device, 8)
    return fs % 4, ((dp >> 1) & 1) * 2 + (fs >> 2), dp >> 2, dp & 1


def device_at(x, y, z, c):
    x, y, z = x % 4, y % 4, z % 8
    return (z * 4 + (y >> 1) * 2 + c) * 8 + (y & 1) * 4 + x


def come_from(array, dx=0, dy=0, dz=0, dc=0):
    pairs = []
    for target in range(DEVICES):
        x, y, z, c = place_of(target)
        pairs.append((device_at(x + dx, y + dy, z + dz, c ^ dc), target))
    return lax.ppermute(array, AXES, pairs)


def here():
    dp, fs = lax.axis_index("dp"), lax.axis_index("fsdp")
    return fs % 4, ((dp // 2) % 2) * 2 + fs // 4, dp // 4, dp % 2


def normalise(values, gain, shift):
    centre = jnp.mean(values, axis=-1, keepdims=True)
    spread = jnp.mean((values - centre) ** 2, axis=-1, keepdims=True)
    return (values - centre) * lax.rsqrt(spread + 1e-06) * gain + shift


BLOCK = 128


def mlp_term(normed, up, bias, down):
    pre = (
        lax.dot_general(normed, up, (((1,), (1,)), ((), ())), preferred_element_type=jnp.float32)
        + bias
    )
    act = jax.nn.gelu(pre, approximate=True).astype(jnp.bfloat16)
    return jnp.dot(act, down, preferred_element_type=jnp.float32)


def over_blocks(tokens, body):
    def step(i, carry):
        body(pl.ds(pl.multiple_of(i * BLOCK, BLOCK), BLOCK), i)
        return carry

    lax.fori_loop(0, tokens // BLOCK, step, 0)


def first_kernel(hidden, gain, shift, up, bias, down, normed, total):
    def body(rows, _):
        flat = hidden[rows].astype(jnp.float32)
        here = normalise(flat, gain[...].reshape(1, -1), shift[...].reshape(1, -1)).astype(
            jnp.bfloat16
        )
        normed[rows] = here
        total[rows] = mlp_term(here, up[...], bias[...], down[...])

    over_blocks(hidden.shape[0], body)


def piece_copies(count, mine, other, up, down, sems):
    core = here()[3]

    def copies(k, first, second):
        rows = pl.ds(k * HALF, HALF)
        return (
            pltpu.make_async_copy(first, up.at[rows], sems.at[k, 0]),
            pltpu.make_async_copy(second, down.at[rows], sems.at[k, 1]),
        )

    @pl.when(core == 0)
    def _():
        for k in range(count):
            for copy in copies(k, mine[k], other[k]):
                copy.start()

    @pl.when(core == 1)
    def _():
        for k in range(count):
            for copy in copies(k, other[k], mine[k]):
                copy.start()

    return [copy for k in range(count) for copy in copies(k, mine[k], other[k])]


def middle_kernel(count, *refs):
    normed_hbm, before_hbm, bias = refs[:3]
    mine, other = refs[3 : 3 + count], refs[3 + count : 3 + 2 * count]
    total, up, down, sems, normed, before, more = refs[3 + 2 * count :]
    waits = piece_copies(count, mine, other, up, down, sems)
    for k, (source, target) in enumerate(((normed_hbm, normed), (before_hbm, before))):
        copy = pltpu.make_async_copy(source, target, more.at[k])
        copy.start()
        waits.append(copy)
    for copy in waits:
        copy.wait()

    def body(rows, _):
        before[rows] = before[rows] + mlp_term(normed[rows], up[...], bias[...], down[...])
        pltpu.make_async_copy(before.at[rows], total.at[rows], more.at[2]).start()

    over_blocks(before.shape[0], body)
    pltpu.make_async_copy(before, total, more.at[2]).wait()


def last_kernel(count, *refs):
    fc2_bias, gain, shift, keep, head_bias, bias = refs[:6]
    normed_hbm, before_hbm, hidden_hbm, head_hbm = refs[6:10]
    mine, other = refs[10 : 10 + count], refs[10 + count : 10 + 2 * count]
    unit, up, down, sems, normed, before, hidden, head, pooled, more = refs[10 + 2 * count :]
    waits = piece_copies(count, mine, other, up, down, sems)
    pairs = (
        (normed_hbm, normed),
        (before_hbm, before),
        (hidden_hbm, hidden),
        (head_hbm, head),
    )
    for k, (source, target) in enumerate(pairs):
        copy = pltpu.make_async_copy(source, target, more.at[k])
        copy.start()
        waits.append(copy)
    for copy in waits[:-1]:
        copy.wait()
    width = unit.shape[1]
    seq = before.shape[0] // unit.shape[0]
    texts = BLOCK // seq

    def body(rows, i):
        mixed = before[rows] + mlp_term(normed[rows], up[...], bias[...], down[...])
        out = hidden[rows].astype(jnp.float32) + mixed + fc2_bias[...].reshape(1, -1)
        final = normalise(out, gain[...].reshape(1, -1), shift[...].reshape(1, -1))
        kept = keep[rows]
        summed = jnp.sum((final * kept).reshape(texts, seq, width), axis=1)
        number = jnp.sum(
            jnp.broadcast_to(kept, (texts * seq, 128)).reshape(texts, seq, 128), axis=1
        )
        pooled[pl.ds(pl.multiple_of(i * texts, texts), texts)] = summed / number[:, :1]

    over_blocks(before.shape[0], body)
    waits[-1].wait()
    emb = jnp.dot(
        pooled[...].astype(jnp.bfloat16), head[...], preferred_element_type=jnp.float32
    ) + head_bias[...].reshape(1, -1)
    unit[...] = (emb * lax.rsqrt(jnp.sum(emb * emb, axis=-1, keepdims=True) + 1e-06)).astype(
        jnp.bfloat16
    )


NEAR = (0, 1, -1, 2)
ROWS = tuple((dy, dc) for dc in (0, 1) for dy in NEAR)


def score_kernel(scalars, *refs):
    rows, images, tiles = refs[:8], refs[8:12], refs[12:16]
    grads, texts, pictures, sems = refs[16:20], refs[20], refs[21], refs[22]
    x, y, _, c = here()
    column = (y // 2) * 2 + c
    size, width = images[0].shape
    copies = []
    for r, (dy, dc) in enumerate(ROWS):
        there_y = (y + dy + 4) % 4
        there_c = (c + dc) % 2
        block = (there_y // 2) * 2 + there_c
        for e, dx in enumerate(NEAR):
            slot = block * 8 + (there_y % 2) * 4 + (x + dx + 4) % 4
            start = pl.multiple_of(slot * size, size)
            copy = pltpu.make_async_copy(
                rows[r].at[pl.ds(e * size, size)], texts.at[pl.ds(start, size)], sems.at[r, e]
            )
            copy.start()
            copies.append(copy)
    for d in range(4):
        pictures[pl.ds(d * size, size)] = images[d][...]
    for copy in copies:
        copy.wait()
    scale, offset = scalars[0], scalars[1]
    pics = pictures[...]
    group = 8 * size
    total = jnp.zeros((4 * size, width), jnp.float32)
    far = lax.broadcasted_iota(jnp.int32, (4 * size, group), 0) // size
    for m in range(4):
        block = (column // 2 + m // 2) % 2 * 2 + (column % 2 + m % 2) % 2
        units = texts[pl.ds(pl.multiple_of(block * group, group), group)]
        score = (
            scale
            * lax.dot_general(
                pics, units, (((1,), (1,)), ((), ())), preferred_element_type=jnp.float32
            )
            + offset
        )
        target = tiles[m][...].reshape(4 * size, group).astype(jnp.float32)
        step = 4 * far + (column - block)
        weight = jnp.where(
            (step >= 0) & (step < 12), jax.nn.sigmoid(score) - jax.nn.sigmoid(target), 0.0
        ).astype(jnp.bfloat16)
        total = total + jnp.dot(weight, units, preferred_element_type=jnp.float32)
    for d in range(4):
        grads[d][...] = total[d * size : (d + 1) * size].astype(grads[d].dtype)


VMEM = pl.BlockSpec(memory_space=pltpu.VMEM)
ANY = pl.BlockSpec(memory_space=pl.ANY)
SMEM = pl.BlockSpec(memory_space=pltpu.SMEM)


def mlp_scratch(count, width):
    return [
        pltpu.VMEM((count * HALF, width), jnp.bfloat16),
        pltpu.VMEM((count * HALF, width), jnp.bfloat16),
        pltpu.SemaphoreType.DMA((count, 2)),
    ]


def after(values, *others):
    return lax.optimization_barrier((values, others))[0]


def on_device(
    hidden,
    text_ids,
    ln_gain,
    ln_bias,
    fc1_weight,
    fc1_bias,
    fc2_weight,
    fc2_bias,
    final_gain,
    final_bias,
    head_weight,
    head_bias,
    image_emb,
    teacher_logits,
    logit_scale,
    logit_bias,
):
    tokens, width = hidden.shape
    texts_here, _ = text_ids.shape
    hidden_here = fc1_weight.shape[1]
    x, y, z, c = here()
    odd = z % 2

    up, down = fc1_weight.T, fc2_weight
    own = jnp.pad(jnp.where(c == 0, up, down), ((0, 2 * HALF - hidden_here), (0, 0)))
    own_p = lax.dynamic_slice_in_dim(own, odd * HALF, HALF, 0)
    own_q = lax.dynamic_slice_in_dim(own, (1 - odd) * HALF, HALF, 0)

    right_p = come_from(own_p, dx=1)
    left_p = come_from(own_p, dx=-1)
    flip_p = come_from(own_p, dy=1)
    flip_q = come_from(own_q, dy=-1)

    shards = fc1_bias.shape[0] // hidden_here
    biases = fc1_bias.reshape(shards, hidden_here)
    own_bias = lax.dynamic_slice_in_dim(biases, (y % 2) * 4 + x, 1, 0)
    halves = jnp.pad(biases, ((0, 0), (0, 2 * HALF - hidden_here))).reshape(2 * shards, HALF)

    def bias_of(wave):
        places = [
            (((y + dy) % 2) * 4 + (x + dx + 4) % 4) * 2 + (odd + other) % 2
            for dx, dy, other in wave
        ]
        return jnp.concatenate(
            [lax.dynamic_slice_in_dim(halves, p, 1, 0) for p in places], axis=1
        )

    normed, total = pl.pallas_call(
        first_kernel,
        out_shape=(
            jax.ShapeDtypeStruct((tokens, width), jnp.bfloat16),
            jax.ShapeDtypeStruct((tokens, width), jnp.float32),
        ),
        in_specs=[VMEM] * 6,
        out_specs=(VMEM, VMEM),
        name="mlp_first",
    )(hidden, ln_gain, ln_bias, up, own_bias, down)

    def add_pieces(total, wave, mine, other):
        count = len(wave)
        return pl.pallas_call(
            functools.partial(middle_kernel, count),
            out_shape=jax.ShapeDtypeStruct((tokens, width), jnp.float32),
            in_specs=[ANY] * 2 + [VMEM] + [ANY] * (2 * count),
            out_specs=ANY,
            scratch_shapes=mlp_scratch(count, width)
            + [
                pltpu.VMEM((tokens, width), jnp.bfloat16),
                pltpu.VMEM((tokens, width), jnp.float32),
                pltpu.SemaphoreType.DMA((3,)),
            ],
            name=f"mlp_middle_{count}",
        )(normed, total, bias_of(wave), *mine, *other)

    def swapped(pieces):
        return [come_from(piece, dc=1) for piece in pieces]

    wave = ((1, 0, 0), (-1, 0, 0), (0, 1, 0), (0, 1, 1))
    right_p, left_p, flip_p, flip_q = mine = after((right_p, left_p, flip_p, flip_q), total)
    right_q = come_from(right_p, dz=1)
    left_q = come_from(left_p, dz=-1)
    flip_right_p = come_from(right_p, dy=1)
    flip_left_p = come_from(left_p, dy=-1)
    over_p = come_from(right_p, dx=1)
    flip_left_q = come_from(flip_q, dx=-1)
    total = add_pieces(total, wave, mine, swapped(mine))

    image_emb, teacher_logits = after((image_emb, teacher_logits), mine)
    images = image_emb.astype(jnp.float32)
    image_unit = (
        images * lax.rsqrt(jnp.sum(images * images, axis=-1, keepdims=True) + 1e-06)
    ).astype(jnp.bfloat16)
    pictures = [image_unit] + [come_from(image_unit, dz=d) for d in (1, 2, 3)]
    column = (y // 2) * 2 + c
    tiles = jnp.pad(jnp.transpose(teacher_logits, (1, 2, 0)), ((3, 4), (0, 0), (0, 0)))
    tile_sets = []
    for m in range(4):
        target = (column // 2 + m // 2) % 2 * 2 + (column % 2 + m % 2) % 2
        part = lax.dynamic_slice_in_dim(tiles, 3 + target - column, 13, 0)[::4]
        tile_sets.append(come_from(part, dy=2 * (m // 2), dc=m % 2) if m else part)
    keep = (text_ids != 0).astype(jnp.float32).reshape(tokens, 1)

    wave = ((1, 0, 1), (-1, 0, 1), (1, 1, 0), (-1, 1, 0), (2, 0, 0), (-1, 1, 1))
    right_q, left_q, flip_right_p, flip_left_p, over_p, flip_left_q = mine = after(
        (right_q, left_q, flip_right_p, flip_left_p, over_p, flip_left_q),
        total,
        pictures,
        tile_sets,
        keep,
    )
    flip_right_q = come_from(flip_right_p, dz=1)
    over_q = come_from(over_p, dz=-1)
    flip_over_p = come_from(over_p, dy=1)
    flip_over_q = come_from(flip_left_q, dx=-1)
    total = add_pieces(total, wave, mine, swapped(mine))

    wave = ((1, 1, 1), (2, 0, 1), (2, 1, 0), (2, 1, 1))
    count = len(wave)
    last_bias = bias_of(wave)
    mine = after((flip_right_q, over_q, flip_over_p, flip_over_q), total, last_bias)
    text_unit = pl.pallas_call(
        functools.partial(last_kernel, count),
        out_shape=jax.ShapeDtypeStruct((texts_here, width), jnp.bfloat16),
        in_specs=[VMEM] * 6 + [ANY] * (4 + 2 * count),
        out_specs=VMEM,
        scratch_shapes=mlp_scratch(count, width)
        + [
            pltpu.VMEM((tokens, width), jnp.bfloat16),
            pltpu.VMEM((tokens, width), jnp.float32),
            pltpu.VMEM((tokens, width), jnp.bfloat16),
            pltpu.VMEM((width, width), jnp.bfloat16),
            pltpu.VMEM((texts_here, width), jnp.float32),
            pltpu.SemaphoreType.DMA((4,)),
        ],
        name="mlp_last",
    )(
        fc2_bias,
        final_gain,
        final_bias,
        keep,
        head_bias,
        last_bias,
        normed,
        total,
        hidden,
        head_weight,
        *mine,
        *swapped(mine),
    )

    near_x = [text_unit] + [come_from(text_unit, dx=d) for d in NEAR[1:]]
    line = jnp.concatenate(near_x, axis=0)
    lines = [line] + [come_from(line, dy=d) for d in NEAR[1:]]
    lines = lines + [come_from(part, dc=1) for part in lines]
    scalars = jnp.concatenate([logit_scale, logit_bias])
    grads = pl.pallas_call(
        score_kernel,
        out_shape=tuple(
            jax.ShapeDtypeStruct((texts_here, width), kind)
            for kind in (jnp.float32, jnp.bfloat16, jnp.bfloat16, jnp.bfloat16)
        ),
        in_specs=[SMEM] + [ANY] * 8 + [VMEM] * 8,
        out_specs=(VMEM,) * 4,
        scratch_shapes=[
            pltpu.VMEM((4 * 8 * texts_here, width), jnp.bfloat16),
            pltpu.VMEM((4 * texts_here, width), jnp.bfloat16),
            pltpu.SemaphoreType.DMA((8, 4)),
        ],
        name="scores",
    )(scalars, *lines, *pictures, *tile_sets)
    total = grads[0]
    for d in (1, 2, 3):
        total = total + come_from(grads[d], dz=-d).astype(jnp.float32)
    return logit_scale[0] * total


def solution(mesh):
    placed = (
        P(("dp", "fsdp"), None),
        P(("dp", "fsdp"), None),
        P(),
        P(),
        P(None, "fsdp"),
        P(),
        P("fsdp", None),
        P(),
        P(),
        P(),
        P(),
        P(),
        P(("dp", "fsdp"), None),
        P("dp", None, "fsdp"),
        P(),
        P(),
    )
    return jax.shard_map(
        on_device, mesh=mesh, in_specs=placed, out_specs=P(("dp", "fsdp"), None), check_vma=False
    )
```

```python
import functools

import jax
import jax.numpy as jnp
from jax import lax
from jax.experimental import pallas as pl
from jax.experimental.pallas import tpu as pltpu
from jax.sharding import PartitionSpec as P


AXES = ("dp", "fsdp")
DEVICES = 256
PART = 136
TILE = 256


def place_of(device):
    dp, fs = divmod(device, 8)
    return fs % 4, ((dp >> 1) & 1) * 2 + (fs >> 2), dp >> 2, dp & 1


def device_at(x, y, z, c):
    x, y, z = x % 4, y % 4, z % 8
    return (z * 4 + (y >> 1) * 2 + c) * 8 + (y & 1) * 4 + x


def come_from(array, dx=0, dy=0, dz=0, dc=0):
    pairs = []
    for target in range(DEVICES):
        x, y, z, c = place_of(target)
        pairs.append((device_at(x + dx, y + dy, z + dz, c ^ dc), target))
    return lax.ppermute(array, AXES, pairs)


def here():
    dp, fs = lax.axis_index("dp"), lax.axis_index("fsdp")
    return fs % 4, ((dp // 2) % 2) * 2 + fs // 4, dp // 4, dp % 2


def normalise(values, gain, shift):
    centre = jnp.mean(values, axis=-1, keepdims=True)
    spread = jnp.mean((values - centre) ** 2, axis=-1, keepdims=True)
    return (values - centre) * lax.rsqrt(spread + 1e-06) * gain + shift


BLOCK = 128
ROWS_STEP = 256


def over_blocks(tokens, body):
    def step(i, carry):
        body(pl.ds(pl.multiple_of(i * BLOCK, BLOCK), BLOCK), i)
        return carry

    lax.fori_loop(0, tokens // BLOCK, step, 0)


def norm_kernel(hidden, gain, shift, normed):
    def body(rows, _):
        normed[rows] = normalise(
            hidden[rows].astype(jnp.float32), gain[...].reshape(1, -1), shift[...].reshape(1, -1)
        ).astype(jnp.bfloat16)

    over_blocks(hidden.shape[0], body)


def hidden_units(normed, up, bias):
    pre = (
        lax.dot_general(normed, up, (((1,), (1,)), ((), ())), preferred_element_type=jnp.float32)
        + bias
    )
    return jax.nn.gelu(pre, approximate=True).astype(jnp.bfloat16)


def cut(first, last, more=()):
    cuts = {first, last, *more} | {u for u in range(first, last) if u % PART == 0}
    cuts = sorted(cuts)
    return [(lo // PART, lo % PART, hi - lo, lo - first) for lo, hi in zip(cuts, cuts[1:])]


def assemble(first, last, parts, up, down):
    skipped = first // PART
    for part, row, rows, unit in cut(first, last):
        ref = parts[part - skipped]
        up[pl.ds(unit, rows)] = ref[pl.ds(row, rows)]
        down[pl.ds(unit, rows)] = ref[pl.ds(PART + row, rows)]


def bias_kernel(shard, places, flat, tiles, line, quarters):
    x, y, z, c = here()
    line[...] = flat[...].reshape(1, -1)
    quarters[...] = jnp.zeros(quarters.shape, quarters.dtype)
    for s in range(flat.shape[0] // shard):
        for q in range(4):
            size = min(PART, shard - q * PART)
            quarters[pl.ds(4 * s + q, 1), pl.ds(0, size)] = line[
                :, pl.ds(s * shard + q * PART, size)
            ]
    tiles[...] = jnp.zeros(tiles.shape, tiles.dtype)
    for part, row, rows, unit in cut(0, len(places) * PART, range(0, len(places) * PART, TILE)):
        dx, dy, other = places[part]
        place = (((y + dy) % 2) * 4 + (x + dx + 4) % 4) * 4 + 2 * c + (z + other) % 2
        values = quarters[pl.ds(place, 1), :]
        tiles[pl.ds(unit // TILE, 1), pl.ds(unit % TILE, rows)] = values[:, row : row + rows]


def part_kernel(ups, downs, *refs):
    outs, sems = refs[:2], refs[2]
    _, _, z, c = here()
    size = ups.shape[0]
    full, rest = (size - 3 * PART) // 8 * 8, (size - 3 * PART) % 8
    for k, out in enumerate(outs):
        quarter = 2 * c + (z + k) % 2

        @pl.when(quarter < 3)
        def _(k=k, out=out, quarter=quarter):
            for side, weight in enumerate((ups, downs)):
                rows = pl.ds(pl.multiple_of(quarter * PART, 8), PART)
                pltpu.make_async_copy(
                    weight.at[rows], out.at[pl.ds(side * PART, PART)], sems.at[k, side]
                ).start()
            for side, weight in enumerate((ups, downs)):
                pltpu.make_async_copy(
                    weight.at[pl.ds(0, PART)], out.at[pl.ds(side * PART, PART)], sems.at[k, side]
                ).wait()

        @pl.when(quarter == 3)
        def _(k=k, out=out):
            copies = []
            for side, weight in enumerate((ups, downs)):
                last = side * PART + full
                out[pl.ds(last, PART - full)] = jnp.zeros((PART - full, out.shape[1]), out.dtype)
                for j, (row, count) in enumerate(((0, full), (full, rest))):
                    copies.append(
                        pltpu.make_async_copy(
                            weight.at[pl.ds(3 * PART + row, count)],
                            out.at[pl.ds(side * PART + row, count)],
                            sems.at[k, 2 + 2 * side + j],
                        )
                    )
            for copy in copies:
                copy.start()
            for copy in copies:
                copy.wait()


def add_kernel(first, last, fresh, count, *refs):
    normed, bias = refs[:2], refs[2]
    before, rest = (refs[3:4], refs[4:]) if fresh else (refs[3:5], refs[5:])
    parts, totals = rest[:count], rest[count : count + 2]
    up, down = rest[-2:]
    if fresh:
        rest[count + 2][...] = (before[0][...] != 0).astype(jnp.float32)
    assemble(first, last, parts, up, down)
    blocks = normed[0].shape[0] // ROWS_STEP

    def step(tile, source):
        units = pl.ds(pl.multiple_of(tile * TILE, TILE), TILE)

        def rows_step(i, carry):
            rows = pl.ds(pl.multiple_of(i * ROWS_STEP, ROWS_STEP), ROWS_STEP)
            for k in range(2):
                act = hidden_units(normed[k][rows], up[units], bias[pl.ds(first // TILE + tile, 1)])
                term = jnp.dot(act, down[units], preferred_element_type=jnp.float32)
                totals[k][rows] = term if source is None else source[k][rows] + term
            return carry

        lax.fori_loop(0, blocks, rows_step, 0)

    def loop_step(tile, carry):
        step(tile, totals)
        return carry

    if fresh:
        step(0, None)
    else:
        lax.fori_loop(0, (last - first) // TILE, loop_step, 0)


def add_tiles(first, last, normed, bias, total, up, down):
    blocks = normed.shape[0] // ROWS_STEP
    steps = (last - first) // TILE
    rest = last - first - steps * TILE

    def rows_step(i, carry):
        rows = pl.ds(pl.multiple_of(i * ROWS_STEP, ROWS_STEP), ROWS_STEP)
        for tile in range(steps + (rest > 0)):
            size = TILE if tile < steps else rest
            units = pl.ds(tile * TILE, size)
            act = hidden_units(normed[rows], up[units], bias[pl.ds(first // TILE + tile, 1)][:, :size])
            total[rows] += jnp.dot(act, down[units], preferred_element_type=jnp.float32)
        return carry

    lax.fori_loop(0, blocks, rows_step, 0)


def finish_other_kernel(first, last, count, *refs):
    normed, bias, _ = refs[:3]
    parts = refs[3 : 3 + count]
    total, up, down = refs[3 + count :]
    assemble(first, last, parts, up, down)
    add_tiles(first, last, normed, bias, total, up, down)


def finish_own_kernel(first, last, normed, bias, before, up, down, hidden, fc2_bias, total):
    def body(rows, _):
        total[rows] = before[rows] + hidden[rows].astype(jnp.float32) + fc2_bias[...].reshape(1, -1)

    over_blocks(before.shape[0], body)
    add_tiles(first, last, normed, bias, total, up, down)


def unit_kernel(here_part, there_part, gain, shift, mask, head, head_bias, unit, pooled):
    width = unit.shape[1]
    seq = here_part.shape[0] // unit.shape[0]
    texts = BLOCK // seq

    def body(rows, i):
        out = here_part[rows] + there_part[rows]
        final = normalise(out, gain[...].reshape(1, -1), shift[...].reshape(1, -1))
        block = pl.ds(pl.multiple_of(i * texts, texts), texts)
        keep = mask[block]
        spread = jnp.broadcast_to(keep[:, None, :], (texts, seq, seq)).reshape(texts * seq, seq)
        at_row = lax.broadcasted_iota(jnp.int32, spread.shape, 0) % seq
        at_lane = lax.broadcasted_iota(jnp.int32, spread.shape, 1)
        kept = jnp.sum(jnp.where(at_row == at_lane, spread, 0.0), axis=1, keepdims=True)
        summed = jnp.sum((final * kept).reshape(texts, seq, width), axis=1)
        pooled[block] = summed / jnp.sum(keep, axis=1, keepdims=True)

    over_blocks(here_part.shape[0], body)
    emb = jnp.dot(
        pooled[...].astype(jnp.bfloat16), head[...], preferred_element_type=jnp.float32
    ) + head_bias[...].reshape(1, -1)
    unit[...] = (emb * lax.rsqrt(jnp.sum(emb * emb, axis=-1, keepdims=True) + 1e-06)).astype(
        jnp.bfloat16
    )


NEAR = (0, 1, 2, -1)
ROWS = tuple((dy, dc) for dc in (0, 1) for dy in NEAR)
TILES = ((0, 0), (2, 0), (1, 0), (2, 4))


def tile_kernel(tiles, own, near, far):
    x, y, _, c = here()
    column = (y // 2) * 2 + c
    _, group = tiles.shape[1:]
    half = group // 2
    for m, (target, at) in enumerate(((own, 0), (near, 0), (far, 0), (far, 4))):
        other = (column // 2 + m // 2) % 2 * 2 + (column % 2 + m % 2) % 2
        for d in range(4):
            step = jnp.clip(4 * d + other - column, 0, tiles.shape[0] - 1)
            tile = tiles[step].astype(jnp.float32)
            parts = [
                pltpu.roll(tile[:, k * half : (k + 1) * half], (4 - x) % 4 * (half // 4), 1)
                for k in range(2)
            ]
            target[at + d] = jnp.concatenate(parts, axis=1).astype(tiles.dtype)


def pack_kernel(near, far, both):
    both[:4] = near[...]
    both[4:] = far[4:]


def score_kernel(logit_scale, logit_bias, *refs):
    lines, images, tiles = refs[:8], refs[8:12], refs[12:15]
    grads, pictures, targets = refs[15:19], refs[19], refs[20]
    _, y, _, c = here()
    column = (y // 2) * 2 + c
    size, width = images[0].shape
    count = lines[0].shape[0]
    for d in range(4):
        pictures[pl.ds(d * size, size)] = images[d][...]
    for m in range(4):
        source, at = TILES[m]
        tile = tiles[source][at : at + 4].reshape(4 * size, 2 * count)
        for k in range(2):
            targets[m, k] = tile[:, k * count : (k + 1) * count]
    scale, offset = logit_scale[0], logit_bias[0]
    pics = pictures[...]
    total = jnp.zeros((4 * size, width), jnp.float32)
    far = lax.broadcasted_iota(jnp.int32, (4 * size, count), 0) // size
    for r, (dy, dc) in enumerate(ROWS):
        there = (y + dy + 4) % 4
        block = (there // 2) * 2 + (c + dc) % 2
        m = (there // 2 + y // 2) % 2 * 2 + dc
        units = lines[r][...]
        score = (
            scale
            * lax.dot_general(
                pics, units, (((1,), (1,)), ((), ())), preferred_element_type=jnp.float32
            )
            + offset
        )
        target = targets[m, there % 2].astype(jnp.float32)
        step = 4 * far + (column - block)
        weight = jnp.where(
            (step >= 0) & (step < 12), jax.nn.sigmoid(score) - jax.nn.sigmoid(target), 0.0
        ).astype(jnp.bfloat16)
        total = total + jnp.dot(weight, units, preferred_element_type=jnp.float32)
    for d in range(4):
        grads[d][...] = total[d * size : (d + 1) * size].astype(grads[d].dtype)


VMEM = pl.BlockSpec(memory_space=pltpu.VMEM)
ANY = pl.BlockSpec(memory_space=pl.ANY)
SMEM = pl.BlockSpec(memory_space=pltpu.SMEM)


def kernel_of(body, mib=10):
    return functools.partial(
        pl.pallas_call, body, compiler_params=pltpu.CompilerParams(vmem_limit_bytes=mib << 20)
    )


def in_hbm(array):
    return pltpu.with_memory_space_constraint(array, pltpu.HBM)


def after(values, *others):
    return lax.optimization_barrier((values, others))[0]


def on_device(
    hidden,
    text_ids,
    ln_gain,
    ln_bias,
    fc1_weight,
    fc1_bias,
    fc2_weight,
    fc2_bias,
    final_gain,
    final_bias,
    head_weight,
    head_bias,
    image_emb,
    teacher_logits,
    logit_scale,
    logit_bias,
):
    tokens, width = hidden.shape
    texts_here, _ = text_ids.shape
    hidden_here = fc1_weight.shape[1]

    part = pltpu.VMEM((2 * PART, width), jnp.bfloat16)
    own_p, own_q = kernel_of(part_kernel, 4)(
        out_shape=(part, part),
        in_specs=[pl.BlockSpec(memory_space=pltpu.HBM)] * 2,
        out_specs=(VMEM, VMEM),
        scratch_shapes=[pltpu.SemaphoreType.DMA((2, 6))],
        name="parts",
    )(in_hbm(fc1_weight.T), in_hbm(fc2_weight))
    right_p = come_from(own_p, dx=1)
    left_p = come_from(own_p, dx=-1)
    flip_p = come_from(own_p, dy=1)
    flip_q = come_from(own_q, dy=-1)

    places = (
        ((0, 0, 0), (0, 0, 1))
        + ((1, 0, 0), (-1, 0, 0), (0, 1, 0), (0, 1, 1))
        + ((1, 0, 1), (-1, 0, 1), (1, 1, 0), (-1, 1, 0), (2, 0, 0), (-1, 1, 1))
        + ((1, 1, 1), (2, 0, 1), (2, 1, 0), (2, 1, 1))
    )
    shards = fc1_bias.shape[0] // hidden_here
    units = len(places) * PART
    bias = kernel_of(functools.partial(bias_kernel, hidden_here, places), 4)(
        out_shape=pltpu.VMEM((-(-units // TILE), TILE), jnp.float32),
        in_specs=[VMEM],
        out_specs=VMEM,
        scratch_shapes=[
            pltpu.VMEM((1, fc1_bias.shape[0]), jnp.float32),
            pltpu.VMEM((4 * shards, TILE), jnp.float32),
        ],
        name="bias",
    )(fc1_bias)

    wide = pltpu.VMEM((tokens, width), jnp.float32)
    hidden = after(hidden, own_p)
    normed = kernel_of(norm_kernel, 4)(
        out_shape=pltpu.VMEM((tokens, width), jnp.bfloat16),
        in_specs=[VMEM] * 3,
        out_specs=VMEM,
        name="norm",
    )(hidden, ln_gain, ln_bias)
    normed = (normed, come_from(normed, dc=1))

    def scratch(first, last):
        return [pltpu.VMEM((last - first, width), jnp.bfloat16)] * 2

    def add_units(first, last, totals, parts):
        parts = parts[first // PART : -(-last // PART)]
        before = (text_ids,) if totals is None else totals
        keep = (pltpu.VMEM(text_ids.shape, jnp.float32),) if totals is None else ()
        return kernel_of(
            functools.partial(add_kernel, first, last, totals is None, len(parts))
        )(
            out_shape=(wide, wide) + keep,
            in_specs=[VMEM] * (3 + len(before) + len(parts)),
            out_specs=(VMEM,) * (2 + len(keep)),
            scratch_shapes=scratch(first, last),
            input_output_aliases={} if keep else {3: 0, 4: 1},
            name=f"units_{first}_{last}",
        )(*normed, bias, *before, *parts)

    parts = (own_p, own_q)
    *totals, keep = add_units(0, 256, None, parts)

    image_emb = after(image_emb, normed[0])
    images = image_emb.astype(jnp.float32)
    image_unit = (
        images * lax.rsqrt(jnp.sum(images * images, axis=-1, keepdims=True) + 1e-06)
    ).astype(jnp.bfloat16)
    pictures = [image_unit] + [come_from(image_unit, dz=d) for d in (1, 2, 3)]

    wave = after((right_p, left_p, flip_p, flip_q), totals, pictures)
    right_p, left_p, flip_p, flip_q = wave
    parts = parts + wave
    right_q = come_from(right_p, dz=1)
    left_q = come_from(left_p, dz=-1)
    flip_right_p = come_from(right_p, dy=1)
    flip_left_p = come_from(left_p, dy=-1)
    over_p = come_from(right_p, dx=1)
    flip_left_q = come_from(flip_q, dx=-1)
    totals = add_units(256, 768, totals, parts)

    teacher_logits = after(teacher_logits, wave)
    tiles = jnp.transpose(teacher_logits, (1, 2, 0))

    kinds = [pltpu.VMEM((n, *tiles.shape[1:]), tiles.dtype) for n in (4, 4, 8)]
    tiles_own, tiles_near, tiles_far = kernel_of(tile_kernel, 4)(
        out_shape=tuple(kinds), in_specs=[VMEM], out_specs=(VMEM,) * 3, name="tiles"
    )(tiles)
    tiles_far = come_from(tiles_far, dy=2)

    wave = after(
        (right_q, left_q, flip_right_p, flip_left_p, over_p, flip_left_q),
        totals,
        tiles_far,
    )
    right_q, left_q, flip_right_p, flip_left_p, over_p, flip_left_q = wave
    parts = parts + wave
    flip_right_q = come_from(flip_right_p, dz=1)
    over_q = come_from(over_p, dz=-1)
    flip_over_p = come_from(over_p, dy=1)
    flip_over_q = come_from(flip_left_q, dx=-1)
    tiles_swap = kernel_of(pack_kernel, 4)(
        out_shape=pltpu.VMEM(tiles_far.shape, tiles_far.dtype),
        in_specs=[VMEM] * 2,
        out_specs=VMEM,
        name="pack",
    )(tiles_near, after(tiles_far, wave))
    tile_sets = (tiles_own, tiles_far, come_from(tiles_swap, dc=1))
    totals = add_units(768, 1536, totals, parts)

    first, last = 1536, units
    parts = parts + after((flip_right_q, over_q, flip_over_p, flip_over_q), totals, tile_sets)
    parts = parts[first // PART :]

    rows = pltpu.VMEM((last - first, width), jnp.bfloat16)
    partial, up, down = kernel_of(
        functools.partial(finish_other_kernel, first, last, len(parts))
    )(
        out_shape=(wide, rows, rows),
        in_specs=[VMEM] * (3 + len(parts)),
        out_specs=(VMEM,) * 3,
        input_output_aliases={2: 0},
        name="finish_other",
    )(normed[1], bias, totals[1], *parts)
    there_part = come_from(partial, dc=1)
    here_part = kernel_of(functools.partial(finish_own_kernel, first, last))(
        out_shape=wide,
        in_specs=[VMEM] * 7,
        out_specs=VMEM,
        name="finish_own",
    )(normed[0], bias, totals[0], up, down, hidden, fc2_bias)
    text_unit = kernel_of(unit_kernel, 6)(
        out_shape=pltpu.VMEM((texts_here, width), jnp.bfloat16),
        in_specs=[VMEM] * 7,
        out_specs=VMEM,
        scratch_shapes=[pltpu.VMEM((texts_here, width), jnp.float32)],
        name="unit",
    )(here_part, there_part, final_gain, final_bias, keep, head_weight, head_bias)

    near_x = [text_unit] + [come_from(text_unit, dx=d) for d in NEAR[1:]]
    across = come_from(text_unit, dy=2)
    line = jnp.concatenate(near_x, axis=0)
    across = [across] + [come_from(across, dx=d) for d in NEAR[1:]]
    lines = [line, come_from(line, dy=1), jnp.concatenate(across, axis=0), come_from(line, dy=-1)]
    lines = lines + [come_from(part, dc=1) for part in lines]
    grads = kernel_of(score_kernel, 6)(
        out_shape=tuple(
            pltpu.VMEM((texts_here, width), kind)
            for kind in (jnp.float32, jnp.bfloat16, jnp.bfloat16, jnp.bfloat16)
        ),
        in_specs=[SMEM] * 2 + [VMEM] * 15,
        out_specs=(VMEM,) * 4,
        scratch_shapes=[
            pltpu.VMEM((4 * texts_here, width), jnp.bfloat16),
            pltpu.VMEM((4, 2, 4 * texts_here, 4 * texts_here), jnp.bfloat16),
        ],
        name="scores",
    )(logit_scale, logit_bias, *lines, *pictures, *tile_sets)
    total = grads[0]
    for d in (1, 2, 3):
        total = total + come_from(grads[d], dz=-d).astype(jnp.float32)
    return logit_scale[0] * total


def solution(mesh):
    placed = (
        P(("dp", "fsdp"), None),
        P(("dp", "fsdp"), None),
        P(),
        P(),
        P(None, "fsdp"),
        P(),
        P("fsdp", None),
        P(),
        P(),
        P(),
        P(),
        P(),
        P(("dp", "fsdp"), None),
        P("dp", None, "fsdp"),
        P(),
        P(),
    )
    return jax.shard_map(
        on_device, mesh=mesh, in_specs=placed, out_specs=P(("dp", "fsdp"), None), check_vma=False
    )
```

```python
import functools

import jax
import jax.numpy as jnp
from jax import lax
from jax.experimental import pallas as pl
from jax.experimental.pallas import tpu as pltpu
from jax.sharding import PartitionSpec as P


AXES = ("dp", "fsdp")
DEVICES = 256
PART = 136
TILE = 256


def place_of(device):
    dp, fs = divmod(device, 8)
    return fs % 4, ((dp >> 1) & 1) * 2 + (fs >> 2), dp >> 2, dp & 1


def device_at(x, y, z, c):
    x, y, z = x % 4, y % 4, z % 8
    return (z * 4 + (y >> 1) * 2 + c) * 8 + (y & 1) * 4 + x


def come_from(array, dx=0, dy=0, dz=0, dc=0):
    pairs = []
    for target in range(DEVICES):
        x, y, z, c = place_of(target)
        pairs.append((device_at(x + dx, y + dy, z + dz, c ^ dc), target))
    return lax.ppermute(array, AXES, pairs)


def here():
    dp, fs = lax.axis_index("dp"), lax.axis_index("fsdp")
    return fs % 4, ((dp // 2) % 2) * 2 + fs // 4, dp // 4, dp % 2


def normalise(values, gain, shift):
    centre = jnp.mean(values, axis=-1, keepdims=True)
    spread = jnp.mean((values - centre) ** 2, axis=-1, keepdims=True)
    return (values - centre) * lax.rsqrt(spread + 1e-06) * gain + shift


BLOCK = 128
ROWS_STEP = 512
SHORT_STEP = 256


def over_blocks(tokens, body):
    def step(i, carry):
        body(pl.ds(pl.multiple_of(i * BLOCK, BLOCK), BLOCK), i)
        return carry

    lax.fori_loop(0, tokens // BLOCK, step, 0)


def norm_kernel(hidden, gain, shift, normed):
    def body(rows, _):
        normed[rows] = normalise(
            hidden[rows].astype(jnp.float32), gain[...].reshape(1, -1), shift[...].reshape(1, -1)
        ).astype(jnp.bfloat16)

    over_blocks(hidden.shape[0], body)


def hidden_units(normed, up, bias):
    pre = (
        lax.dot_general(normed, up, (((1,), (1,)), ((), ())), preferred_element_type=jnp.float32)
        + bias
    )
    return jax.nn.gelu(pre, approximate=True).astype(jnp.bfloat16)


def cut(first, last, more=()):
    cuts = {first, last, *more} | {u for u in range(first, last) if u % PART == 0}
    cuts = sorted(cuts)
    return [(lo // PART, lo % PART, hi - lo, lo - first) for lo, hi in zip(cuts, cuts[1:])]


def assemble(first, last, parts, up, down):
    skipped = first // PART
    for part, row, rows, unit in cut(first, last):
        ref = parts[part - skipped]
        up[pl.ds(unit, rows)] = ref[pl.ds(row, rows)]
        down[pl.ds(unit, rows)] = ref[pl.ds(PART + row, rows)]


def bias_kernel(shard, places, flat, tiles, line, quarters):
    x, y, z, c = here()
    line[...] = flat[...].reshape(1, -1)
    quarters[...] = jnp.zeros(quarters.shape, quarters.dtype)
    for s in range(flat.shape[0] // shard):
        for q in range(4):
            size = min(PART, shard - q * PART)
            quarters[pl.ds(4 * s + q, 1), pl.ds(0, size)] = line[
                :, pl.ds(s * shard + q * PART, size)
            ]
    tiles[...] = jnp.zeros(tiles.shape, tiles.dtype)
    for part, row, rows, unit in cut(0, len(places) * PART, range(0, len(places) * PART, TILE)):
        dx, dy, other = places[part]
        place = (((y + dy) % 2) * 4 + (x + dx + 4) % 4) * 4 + 2 * c + (z + other) % 2
        values = quarters[pl.ds(place, 1), :]
        tiles[pl.ds(unit // TILE, 1), pl.ds(unit % TILE, rows)] = values[:, row : row + rows]


def part_kernel(ups, downs, *refs):
    outs, sems = refs[:2], refs[2]
    _, _, z, c = here()
    size = ups.shape[0]
    full, rest = (size - 3 * PART) // 8 * 8, (size - 3 * PART) % 8

    def whole(k, row):
        return [
            pltpu.make_async_copy(
                weight.at[pl.ds(row, PART)], outs[k].at[pl.ds(side * PART, PART)], sems.at[k, side]
            )
            for side, weight in enumerate((ups, downs))
        ]

    def short(k):
        return [
            pltpu.make_async_copy(
                weight.at[pl.ds(3 * PART + row, count)],
                outs[k].at[pl.ds(side * PART + row, count)],
                sems.at[k, 2 + 2 * side + j],
            )
            for side, weight in enumerate((ups, downs))
            for j, (row, count) in enumerate(((0, full), (full, rest)))
        ]

    for waiting in (False, True):
        for k, out in enumerate(outs):
            quarter = 2 * c + (z + k) % 2

            @pl.when(quarter < 3)
            def _(k=k, quarter=quarter, waiting=waiting):
                for copy in whole(k, pl.multiple_of(quarter * PART, 8)):
                    copy.wait() if waiting else copy.start()

            @pl.when(quarter == 3)
            def _(k=k, out=out, waiting=waiting):
                if not waiting:
                    for side in range(2):
                        zeros = jnp.zeros((PART - full, out.shape[1]), out.dtype)
                        out[pl.ds(side * PART + full, PART - full)] = zeros
                for copy in short(k):
                    copy.wait() if waiting else copy.start()


def add_term(first, tile, size, rows, normed, bias, up, down):
    units = pl.ds(tile * TILE, size)
    act = hidden_units(normed[rows], up[units], bias[pl.ds(first // TILE + tile, 1)][:, :size])
    return jnp.dot(act, down[units], preferred_element_type=jnp.float32)


def first_kernel(last, own, other, bias, ids, part_p, part_q, normed, total, mask, up, down):
    mask[...] = (ids[...] != 0).astype(jnp.float32)
    count = own.shape[0]
    normed[:count] = own[...]
    normed[count:] = other[...]
    assemble(0, last, (part_p, part_q), up, down)

    def step(i, carry):
        rows = pl.ds(pl.multiple_of(i * SHORT_STEP, SHORT_STEP), SHORT_STEP)
        total[rows] = add_term(0, 0, TILE, rows, normed, bias, up, down)
        return carry

    lax.fori_loop(0, normed.shape[0] // SHORT_STEP, step, 0)


def add_kernel(first, last, count, normed, bias, _, *refs):
    parts, (total, up, down) = refs[:count], refs[count:]
    assemble(first, last, parts, up, down)
    blocks = normed.shape[0] // ROWS_STEP

    def step(i, carry):
        rows = pl.ds(pl.multiple_of(i % blocks * ROWS_STEP, ROWS_STEP), ROWS_STEP)
        total[rows] += add_term(first, i // blocks, TILE, rows, normed, bias, up, down)
        return carry

    lax.fori_loop(0, (last - first) // TILE * blocks, step, 0)


def add_tiles(first, last, base, normed, bias, total, up, down):
    steps = (last - first) // TILE
    rest = last - first - steps * TILE
    tokens = total.shape[0]

    def step(tile, carry):
        total[...] += add_term(first, tile, TILE, pl.ds(base, tokens), normed, bias, up, down)
        return carry

    lax.fori_loop(0, steps, step, 0)

    def rest_step(i, carry):
        start = pl.multiple_of(i * SHORT_STEP, SHORT_STEP)
        rows = pl.ds(base + start, SHORT_STEP)
        total[pl.ds(start, SHORT_STEP)] += add_term(
            first, steps, rest, rows, normed, bias, up, down
        )
        return carry

    if rest:
        lax.fori_loop(0, tokens // SHORT_STEP, rest_step, 0)


def finish_other_kernel(first, last, count, normed, bias, before, *refs):
    parts, (total, up, down) = refs[:count], refs[count:]
    assemble(first, last, parts, up, down)
    tokens = total.shape[0]
    total[...] = before[tokens:]
    add_tiles(first, last, tokens, normed, bias, total, up, down)


def finish_own_kernel(first, last, normed, bias, before, up, down, hidden, fc2_bias, total):
    def body(rows, _):
        total[rows] = before[rows] + hidden[rows].astype(jnp.float32) + fc2_bias[...].reshape(1, -1)

    over_blocks(total.shape[0], body)
    add_tiles(first, last, 0, normed, bias, total, up, down)


def unit_kernel(here_part, there_part, gain, shift, mask, head, head_bias, unit, pooled):
    width = unit.shape[1]
    seq = here_part.shape[0] // unit.shape[0]
    texts = BLOCK // seq

    def body(rows, i):
        out = here_part[rows] + there_part[rows]
        final = normalise(out, gain[...].reshape(1, -1), shift[...].reshape(1, -1))
        block = pl.ds(pl.multiple_of(i * texts, texts), texts)
        keep = mask[block]
        spread = jnp.broadcast_to(keep[:, None, :], (texts, seq, seq)).reshape(texts * seq, seq)
        at_row = lax.broadcasted_iota(jnp.int32, spread.shape, 0) % seq
        at_lane = lax.broadcasted_iota(jnp.int32, spread.shape, 1)
        kept = jnp.sum(jnp.where(at_row == at_lane, spread, 0.0), axis=1, keepdims=True)
        summed = jnp.sum((final * kept).reshape(texts, seq, width), axis=1)
        pooled[block] = summed / jnp.sum(keep, axis=1, keepdims=True)

    over_blocks(here_part.shape[0], body)
    emb = jnp.dot(
        pooled[...].astype(jnp.bfloat16), head[...], preferred_element_type=jnp.float32
    ) + head_bias[...].reshape(1, -1)
    unit[...] = (emb * lax.rsqrt(jnp.sum(emb * emb, axis=-1, keepdims=True) + 1e-06)).astype(
        jnp.bfloat16
    )


NEAR = (0, 1, 2, -1)
ROWS = tuple((dy, dc) for dc in (0, 1) for dy in NEAR)
TILES = ((0, 0), (2, 0), (1, 0), (2, 4))


def tile_kernel(tiles, own, near, far):
    x, y, _, c = here()
    column = (y // 2) * 2 + c
    _, group = tiles.shape[1:]
    half = group // 2
    for m, (target, at) in enumerate(((own, 0), (near, 0), (far, 0), (far, 4))):
        other = (column // 2 + m // 2) % 2 * 2 + (column % 2 + m % 2) % 2
        for d in range(4):
            step = jnp.clip(4 * d + other - column, 0, tiles.shape[0] - 1)
            tile = tiles[step].astype(jnp.float32)
            parts = [
                pltpu.roll(tile[:, k * half : (k + 1) * half], (4 - x) % 4 * (half // 4), 1)
                for k in range(2)
            ]
            target[at + d] = jnp.concatenate(parts, axis=1).astype(tiles.dtype)


def pack_kernel(near, far, both):
    both[:4] = near[...]
    both[4:] = far[4:]


def score_kernel(logit_scale, logit_bias, *refs):
    lines, images, tiles = refs[:8], refs[8:12], refs[12:15]
    grads, pictures, targets = refs[15:19], refs[19], refs[20]
    _, y, _, c = here()
    column = (y // 2) * 2 + c
    size, width = images[0].shape
    count = lines[0].shape[0]
    for d in range(4):
        pictures[pl.ds(d * size, size)] = images[d][...]
    for m in range(4):
        source, at = TILES[m]
        tile = tiles[source][at : at + 4].reshape(4 * size, 2 * count)
        for k in range(2):
            targets[m, k] = tile[:, k * count : (k + 1) * count]
    scale, offset = logit_scale[0], logit_bias[0]
    pics = pictures[...]
    total = jnp.zeros((4 * size, width), jnp.float32)
    far = lax.broadcasted_iota(jnp.int32, (4 * size, count), 0) // size
    for r, (dy, dc) in enumerate(ROWS):
        there = (y + dy + 4) % 4
        block = (there // 2) * 2 + (c + dc) % 2
        m = (there // 2 + y // 2) % 2 * 2 + dc
        units = lines[r][...]
        score = (
            scale
            * lax.dot_general(
                pics, units, (((1,), (1,)), ((), ())), preferred_element_type=jnp.float32
            )
            + offset
        )
        target = targets[m, there % 2].astype(jnp.float32)
        step = 4 * far + (column - block)
        weight = jnp.where(
            (step >= 0) & (step < 12), jax.nn.sigmoid(score) - jax.nn.sigmoid(target), 0.0
        ).astype(jnp.bfloat16)
        total = total + jnp.dot(weight, units, preferred_element_type=jnp.float32)
    for d in range(4):
        grads[d][...] = total[d * size : (d + 1) * size].astype(grads[d].dtype)


VMEM = pl.BlockSpec(memory_space=pltpu.VMEM)
ANY = pl.BlockSpec(memory_space=pl.ANY)
SMEM = pl.BlockSpec(memory_space=pltpu.SMEM)


def kernel_of(body, mib=10):
    return functools.partial(
        pl.pallas_call, body, compiler_params=pltpu.CompilerParams(vmem_limit_bytes=mib << 20)
    )


def in_hbm(array):
    return pltpu.with_memory_space_constraint(array, pltpu.HBM)


def after(values, *others):
    return lax.optimization_barrier((values, others))[0]


def on_device(
    hidden,
    text_ids,
    ln_gain,
    ln_bias,
    fc1_weight,
    fc1_bias,
    fc2_weight,
    fc2_bias,
    final_gain,
    final_bias,
    head_weight,
    head_bias,
    image_emb,
    teacher_logits,
    logit_scale,
    logit_bias,
):
    tokens, width = hidden.shape
    texts_here, _ = text_ids.shape
    hidden_here = fc1_weight.shape[1]

    part = pltpu.VMEM((2 * PART, width), jnp.bfloat16)
    own_p, own_q = kernel_of(part_kernel, 4)(
        out_shape=(part, part),
        in_specs=[pl.BlockSpec(memory_space=pltpu.HBM)] * 2,
        out_specs=(VMEM, VMEM),
        scratch_shapes=[pltpu.SemaphoreType.DMA((2, 6))],
        name="parts",
    )(in_hbm(fc1_weight.T), in_hbm(fc2_weight))

    right_p = come_from(own_p, dx=1)
    flip_q = come_from(own_q, dy=-1)
    left_p = come_from(own_p, dx=-1)
    flip_p = come_from(own_p, dy=1)
    over_p = come_from(right_p, dx=1)
    flip_right_p = come_from(right_p, dy=1)
    flip_left_q = come_from(flip_q, dx=-1)

    places = (
        ((0, 0, 0), (0, 0, 1))
        + ((1, 0, 0), (-1, 0, 0), (0, 1, 0), (0, 1, 1))
        + ((1, 0, 1), (-1, 0, 1), (1, 1, 0), (-1, 1, 0), (2, 0, 0), (-1, 1, 1))
        + ((1, 1, 1), (2, 0, 1), (2, 1, 0), (2, 1, 1))
    )
    shards = fc1_bias.shape[0] // hidden_here
    units = len(places) * PART
    bias = kernel_of(functools.partial(bias_kernel, hidden_here, places), 4)(
        out_shape=pltpu.VMEM((-(-units // TILE), TILE), jnp.float32),
        in_specs=[VMEM],
        out_specs=VMEM,
        scratch_shapes=[
            pltpu.VMEM((1, fc1_bias.shape[0]), jnp.float32),
            pltpu.VMEM((4 * shards, TILE), jnp.float32),
        ],
        name="bias",
    )(fc1_bias)

    wide = pltpu.VMEM((tokens, width), jnp.float32)
    hidden = after(hidden, own_p)
    normed = kernel_of(norm_kernel, 4)(
        out_shape=pltpu.VMEM((tokens, width), jnp.bfloat16),
        in_specs=[VMEM] * 3,
        out_specs=VMEM,
        name="norm",
    )(hidden, ln_gain, ln_bias)
    other = come_from(normed, dc=1)
    images = after(image_emb, normed).astype(jnp.float32)
    image_unit = (
        images * lax.rsqrt(jnp.sum(images * images, axis=-1, keepdims=True) + 1e-06)
    ).astype(jnp.bfloat16)
    pictures = [image_unit] + [come_from(image_unit, dz=d) for d in (1, 2, 3)]

    def scratch(first, last):
        return [pltpu.VMEM((last - first, width), jnp.bfloat16)] * 2

    both = pltpu.VMEM((2 * tokens, width), jnp.float32)
    normed, total, keep = kernel_of(functools.partial(first_kernel, TILE))(
        out_shape=(
            pltpu.VMEM((2 * tokens, width), jnp.bfloat16),
            both,
            pltpu.VMEM(text_ids.shape, jnp.float32),
        ),
        in_specs=[VMEM] * 6,
        out_specs=(VMEM,) * 3,
        scratch_shapes=scratch(0, TILE),
        name="units_first",
    )(normed, other, bias, text_ids, own_p, own_q)

    def add_units(first, last, total, parts, name):
        parts = parts[first // PART : -(-last // PART)]
        return kernel_of(functools.partial(add_kernel, first, last, len(parts)))(
            out_shape=both,
            in_specs=[VMEM] * (3 + len(parts)),
            out_specs=VMEM,
            scratch_shapes=scratch(first, last),
            input_output_aliases={2: 0},
            name=name,
        )(normed, bias, total, *parts)

    right_p, left_p, flip_p = after((right_p, left_p, flip_p), total, pictures)
    right_q = come_from(right_p, dz=1)
    left_q = come_from(left_p, dz=-1)
    flip_left_p = come_from(left_p, dy=-1)
    parts = (own_p, own_q, right_p, left_p, flip_p, flip_q)
    total = add_units(TILE, 768, total, parts, "units_second")

    over_p, flip_right_p, flip_left_q = after((over_p, flip_right_p, flip_left_q), total)
    flip_over_q = come_from(flip_left_q, dx=-1)
    flip_right_q = come_from(flip_right_p, dz=1)
    over_q = come_from(over_p, dz=-1)
    flip_over_p = come_from(over_p, dy=1)

    tiles = jnp.transpose(after(teacher_logits, total), (1, 2, 0))
    kinds = [pltpu.VMEM((n, *tiles.shape[1:]), tiles.dtype) for n in (4, 4, 8)]
    tiles_own, tiles_near, tiles_far = kernel_of(tile_kernel, 4)(
        out_shape=tuple(kinds), in_specs=[VMEM], out_specs=(VMEM,) * 3, name="tiles"
    )(tiles)
    tiles_far = come_from(tiles_far, dy=2)

    parts = parts + (right_q, left_q, flip_right_p, flip_left_p, over_p, flip_left_q)
    total = add_units(768, 1536, total, parts, "units_third")

    first, last = 1536, units
    parts = (parts + (flip_right_q, over_q, flip_over_p, flip_over_q))[first // PART :]

    rows = pltpu.VMEM((last - first, width), jnp.bfloat16)
    partial, up, down = kernel_of(
        functools.partial(finish_other_kernel, first, last, len(parts))
    )(
        out_shape=(wide, rows, rows),
        in_specs=[VMEM] * (3 + len(parts)),
        out_specs=(VMEM,) * 3,
        name="finish_other",
    )(normed, bias, total, *parts)
    there_part = come_from(partial, dc=1)
    here_part = kernel_of(functools.partial(finish_own_kernel, first, last))(
        out_shape=wide,
        in_specs=[VMEM] * 7,
        out_specs=VMEM,
        name="finish_own",
    )(normed, bias, total, up, down, hidden, fc2_bias)
    text_unit = kernel_of(unit_kernel, 6)(
        out_shape=pltpu.VMEM((texts_here, width), jnp.bfloat16),
        in_specs=[VMEM] * 7,
        out_specs=VMEM,
        scratch_shapes=[pltpu.VMEM((texts_here, width), jnp.float32)],
        name="unit",
    )(here_part, there_part, final_gain, final_bias, keep, head_weight, head_bias)

    near_x = [text_unit] + [come_from(text_unit, dx=d) for d in NEAR[1:]]
    across = come_from(text_unit, dy=2)
    line = jnp.concatenate(near_x, axis=0)
    across = [across] + [come_from(across, dx=d) for d in NEAR[1:]]
    lines = [line, come_from(line, dy=1), jnp.concatenate(across, axis=0), come_from(line, dy=-1)]
    tiles_near, tiles_far = after((tiles_near, tiles_far), text_unit)
    tiles_swap = kernel_of(pack_kernel, 4)(
        out_shape=pltpu.VMEM(tiles_far.shape, tiles_far.dtype),
        in_specs=[VMEM] * 2,
        out_specs=VMEM,
        name="pack",
    )(tiles_near, tiles_far)
    tile_sets = (tiles_own, tiles_far, come_from(tiles_swap, dc=1))
    lines = lines + [come_from(part, dc=1) for part in lines]
    grads = kernel_of(score_kernel, 6)(
        out_shape=tuple(
            pltpu.VMEM((texts_here, width), kind)
            for kind in (jnp.float32, jnp.bfloat16, jnp.bfloat16, jnp.bfloat16)
        ),
        in_specs=[SMEM] * 2 + [VMEM] * 15,
        out_specs=(VMEM,) * 4,
        scratch_shapes=[
            pltpu.VMEM((4 * texts_here, width), jnp.bfloat16),
            pltpu.VMEM((4, 2, 4 * texts_here, 4 * texts_here), jnp.bfloat16),
        ],
        name="scores",
    )(logit_scale, logit_bias, *lines, *pictures, *tile_sets)
    total = grads[0]
    for d in (1, 2, 3):
        total = total + come_from(grads[d], dz=-d).astype(jnp.float32)
    return logit_scale[0] * total


def solution(mesh):
    placed = (
        P(("dp", "fsdp"), None),
        P(("dp", "fsdp"), None),
        P(),
        P(),
        P(None, "fsdp"),
        P(),
        P("fsdp", None),
        P(),
        P(),
        P(),
        P(),
        P(),
        P(("dp", "fsdp"), None),
        P("dp", None, "fsdp"),
        P(),
        P(),
    )
    return jax.shard_map(
        on_device, mesh=mesh, in_specs=placed, out_specs=P(("dp", "fsdp"), None), check_vma=False
    )
```

```python
import functools

import jax
import jax.numpy as jnp
from jax import lax
from jax.experimental import pallas as pl
from jax.experimental.pallas import tpu as pltpu
from jax.sharding import PartitionSpec as P


AXES = ("dp", "fsdp")
DEVICES = 256
PART = 136
TILE = 256


def place_of(device):
    dp, fs = divmod(device, 8)
    return fs % 4, ((dp >> 1) & 1) * 2 + (fs >> 2), dp >> 2, dp & 1


def device_at(x, y, z, c):
    x, y, z = x % 4, y % 4, z % 8
    return (z * 4 + (y >> 1) * 2 + c) * 8 + (y & 1) * 4 + x


def come_from(array, dx=0, dy=0, dz=0, dc=0):
    pairs = []
    for target in range(DEVICES):
        x, y, z, c = place_of(target)
        pairs.append((device_at(x + dx, y + dy, z + dz, c ^ dc), target))
    return lax.ppermute(array, AXES, pairs)


def here():
    dp, fs = lax.axis_index("dp"), lax.axis_index("fsdp")
    return fs % 4, ((dp // 2) % 2) * 2 + fs // 4, dp // 4, dp % 2


def normalise(values, gain, shift):
    centre = jnp.mean(values, axis=-1, keepdims=True)
    spread = jnp.mean((values - centre) ** 2, axis=-1, keepdims=True)
    return (values - centre) * lax.rsqrt(spread + 1e-06) * gain + shift


BLOCK = 128
ROWS_STEP = 256


def over_blocks(tokens, body):
    def step(i, carry):
        body(pl.ds(pl.multiple_of(i * BLOCK, BLOCK), BLOCK), i)
        return carry

    lax.fori_loop(0, tokens // BLOCK, step, 0)


def norm_kernel(hidden, gain, shift, normed):
    def body(rows, _):
        normed[rows] = normalise(
            hidden[rows].astype(jnp.float32), gain[...].reshape(1, -1), shift[...].reshape(1, -1)
        ).astype(jnp.bfloat16)

    over_blocks(hidden.shape[0], body)


def hidden_units(normed, up, bias):
    pre = (
        lax.dot_general(normed, up, (((1,), (1,)), ((), ())), preferred_element_type=jnp.float32)
        + bias
    )
    return jax.nn.gelu(pre, approximate=True).astype(jnp.bfloat16)


def cut(first, last, more=()):
    cuts = {first, last, *more} | {u for u in range(first, last) if u % PART == 0}
    cuts = sorted(cuts)
    return [(lo // PART, lo % PART, hi - lo, lo - first) for lo, hi in zip(cuts, cuts[1:])]


def assemble(first, last, parts, up, down):
    skipped = first // PART
    for part, row, rows, unit in cut(first, last):
        ref = parts[part - skipped]
        up[pl.ds(unit, rows)] = ref[pl.ds(row, rows)]
        down[pl.ds(unit, rows)] = ref[pl.ds(PART + row, rows)]


def bias_kernel(shard, places, flat, tiles, line, quarters):
    x, y, z, c = here()
    line[...] = flat[...].reshape(1, -1)
    quarters[...] = jnp.zeros(quarters.shape, quarters.dtype)
    for s in range(flat.shape[0] // shard):
        for q in range(4):
            size = min(PART, shard - q * PART)
            quarters[pl.ds(4 * s + q, 1), pl.ds(0, size)] = line[
                :, pl.ds(s * shard + q * PART, size)
            ]
    tiles[...] = jnp.zeros(tiles.shape, tiles.dtype)
    for part, row, rows, unit in cut(0, len(places) * PART, range(0, len(places) * PART, TILE)):
        dx, dy, other = places[part]
        place = (((y + dy) % 2) * 4 + (x + dx + 4) % 4) * 4 + 2 * c + (z + other) % 2
        values = quarters[pl.ds(place, 1), :]
        tiles[pl.ds(unit // TILE, 1), pl.ds(unit % TILE, rows)] = values[:, row : row + rows]


def part_kernel(ups, downs, *refs):
    outs, sems = refs[:2], refs[2]
    _, _, z, c = here()
    size = ups.shape[0]
    full, rest = (size - 3 * PART) // 8 * 8, (size - 3 * PART) % 8

    def whole(k, row):
        return [
            pltpu.make_async_copy(
                weight.at[pl.ds(row, PART)], outs[k].at[pl.ds(side * PART, PART)], sems.at[k, side]
            )
            for side, weight in enumerate((ups, downs))
        ]

    def short(k):
        return [
            pltpu.make_async_copy(
                weight.at[pl.ds(3 * PART + row, count)],
                outs[k].at[pl.ds(side * PART + row, count)],
                sems.at[k, 2 + 2 * side + j],
            )
            for side, weight in enumerate((ups, downs))
            for j, (row, count) in enumerate(((0, full), (full, rest)))
        ]

    for waiting in (False, True):
        for k, out in enumerate(outs):
            quarter = 2 * c + (z + k) % 2

            @pl.when(quarter < 3)
            def _(k=k, quarter=quarter, waiting=waiting):
                for copy in whole(k, pl.multiple_of(quarter * PART, 8)):
                    copy.wait() if waiting else copy.start()

            @pl.when(quarter == 3)
            def _(k=k, out=out, waiting=waiting):
                if not waiting:
                    for side in range(2):
                        zeros = jnp.zeros((PART - full, out.shape[1]), out.dtype)
                        out[pl.ds(side * PART + full, PART - full)] = zeros
                for copy in short(k):
                    copy.wait() if waiting else copy.start()


def add_tiles(first, last, base, normed, bias, before, total, up, down):
    step_rows = min(total.shape[0], ROWS_STEP)

    def step(i, carry):
        start = pl.multiple_of(i * step_rows, step_rows)
        rows = pl.ds(base + start, step_rows)
        here = pl.ds(start, step_rows)
        for unit in range(0, last - first, TILE):
            size = min(TILE, last - first - unit)
            units = pl.ds(unit, size)
            tile_bias = bias[pl.ds((first + unit) // TILE, 1)][:, :size]
            act = hidden_units(normed[rows], up[units], tile_bias)
            term = jnp.dot(act, down[units], preferred_element_type=jnp.float32)
            if unit:
                total[here] += term
            else:
                total[here] = term if before is None else before[rows] + term
        return carry

    lax.fori_loop(0, total.shape[0] // step_rows, step, 0)


def first_kernel(last, own, other, bias, ids, part_p, part_q, normed, total, mask, up, down):
    mask[...] = (ids[...] != 0).astype(jnp.float32)
    count = own.shape[0]
    normed[:count] = own[...]
    normed[count:] = other[...]
    assemble(0, last, (part_p, part_q), up, down)
    add_tiles(0, last, 0, normed, bias, None, total, up, down)


def add_kernel(first, last, count, normed, bias, before, *refs):
    parts, (total, up, down) = refs[:count], refs[count:]
    assemble(first, last, parts, up, down)
    add_tiles(first, last, 0, normed, bias, before, total, up, down)


def finish_other_kernel(first, last, count, normed, bias, before, *refs):
    parts, (total, up, down) = refs[:count], refs[count:]
    assemble(first, last, parts, up, down)
    add_tiles(first, last, total.shape[0], normed, bias, before, total, up, down)


def finish_own_kernel(first, last, normed, bias, before, up, down, hidden, fc2_bias, total):
    def body(rows, _):
        total[rows] = before[rows] + hidden[rows].astype(jnp.float32) + fc2_bias[...].reshape(1, -1)

    over_blocks(total.shape[0], body)
    add_tiles(first, last, 0, normed, bias, total, total, up, down)


def unit_kernel(here_part, there_part, gain, shift, mask, head, head_bias, unit, pooled):
    width = unit.shape[1]
    seq = here_part.shape[0] // unit.shape[0]
    texts = BLOCK // seq

    def body(rows, i):
        out = here_part[rows] + there_part[rows]
        final = normalise(out, gain[...].reshape(1, -1), shift[...].reshape(1, -1))
        block = pl.ds(pl.multiple_of(i * texts, texts), texts)
        keep = mask[block]
        spread = jnp.broadcast_to(keep[:, None, :], (texts, seq, seq)).reshape(texts * seq, seq)
        at_row = lax.broadcasted_iota(jnp.int32, spread.shape, 0) % seq
        at_lane = lax.broadcasted_iota(jnp.int32, spread.shape, 1)
        kept = jnp.sum(jnp.where(at_row == at_lane, spread, 0.0), axis=1, keepdims=True)
        summed = jnp.sum((final * kept).reshape(texts, seq, width), axis=1)
        pooled[block] = summed / jnp.sum(keep, axis=1, keepdims=True)

    over_blocks(here_part.shape[0], body)
    emb = jnp.dot(
        pooled[...].astype(jnp.bfloat16), head[...], preferred_element_type=jnp.float32
    ) + head_bias[...].reshape(1, -1)
    unit[...] = (emb * lax.rsqrt(jnp.sum(emb * emb, axis=-1, keepdims=True) + 1e-06)).astype(
        jnp.bfloat16
    )


NEAR = (0, 1, 2, -1)
ROWS = tuple((dy, dc) for dc in (0, 1) for dy in NEAR)
TILES = ((0, 0), (2, 0), (1, 0), (2, 4))


def tile_kernel(tiles, own, near, far):
    x, y, _, c = here()
    column = (y // 2) * 2 + c
    _, group = tiles.shape[1:]
    half = group // 2
    for m, (target, at) in enumerate(((own, 0), (near, 0), (far, 0), (far, 4))):
        other = (column // 2 + m // 2) % 2 * 2 + (column % 2 + m % 2) % 2
        for d in range(4):
            step = jnp.clip(4 * d + other - column, 0, tiles.shape[0] - 1)
            tile = tiles[step].astype(jnp.float32)
            parts = [
                pltpu.roll(tile[:, k * half : (k + 1) * half], (4 - x) % 4 * (half // 4), 1)
                for k in range(2)
            ]
            target[at + d] = jnp.concatenate(parts, axis=1).astype(tiles.dtype)


def pack_kernel(near, far, both):
    both[:4] = near[...]
    both[4:] = far[4:]


def score_kernel(logit_scale, logit_bias, *refs):
    lines, images, tiles = refs[:8], refs[8:12], refs[12:15]
    grads, pictures, targets = refs[15:19], refs[19], refs[20]
    _, y, _, c = here()
    column = (y // 2) * 2 + c
    size, width = images[0].shape
    count = lines[0].shape[0]
    for d in range(4):
        pictures[pl.ds(d * size, size)] = images[d][...]
    for m in range(4):
        source, at = TILES[m]
        tile = tiles[source][at : at + 4].reshape(4 * size, 2 * count)
        for k in range(2):
            targets[m, k] = tile[:, k * count : (k + 1) * count]
    scale, offset = logit_scale[0], logit_bias[0]
    pics = pictures[...]
    total = jnp.zeros((4 * size, width), jnp.float32)
    far = lax.broadcasted_iota(jnp.int32, (4 * size, count), 0) // size
    for r, (dy, dc) in enumerate(ROWS):
        there = (y + dy + 4) % 4
        block = (there // 2) * 2 + (c + dc) % 2
        m = (there // 2 + y // 2) % 2 * 2 + dc
        units = lines[r][...]
        score = (
            scale
            * lax.dot_general(
                pics, units, (((1,), (1,)), ((), ())), preferred_element_type=jnp.float32
            )
            + offset
        )
        target = targets[m, there % 2].astype(jnp.float32)
        step = 4 * far + (column - block)
        weight = jnp.where(
            (step >= 0) & (step < 12), jax.nn.sigmoid(score) - jax.nn.sigmoid(target), 0.0
        ).astype(jnp.bfloat16)
        total = total + jnp.dot(weight, units, preferred_element_type=jnp.float32)
    for d in range(4):
        grads[d][...] = total[d * size : (d + 1) * size].astype(grads[d].dtype)


VMEM = pl.BlockSpec(memory_space=pltpu.VMEM)
ANY = pl.BlockSpec(memory_space=pl.ANY)
SMEM = pl.BlockSpec(memory_space=pltpu.SMEM)


def kernel_of(body, mib=10):
    return functools.partial(
        pl.pallas_call, body, compiler_params=pltpu.CompilerParams(vmem_limit_bytes=mib << 20)
    )


def in_hbm(array):
    return pltpu.with_memory_space_constraint(array, pltpu.HBM)


def after(values, *others):
    return lax.optimization_barrier((values, others))[0]


def on_device(
    hidden,
    text_ids,
    ln_gain,
    ln_bias,
    fc1_weight,
    fc1_bias,
    fc2_weight,
    fc2_bias,
    final_gain,
    final_bias,
    head_weight,
    head_bias,
    image_emb,
    teacher_logits,
    logit_scale,
    logit_bias,
):
    tokens, width = hidden.shape
    texts_here, _ = text_ids.shape
    hidden_here = fc1_weight.shape[1]

    part = pltpu.VMEM((2 * PART, width), jnp.bfloat16)
    own_p, own_q = kernel_of(part_kernel, 4)(
        out_shape=(part, part),
        in_specs=[pl.BlockSpec(memory_space=pltpu.HBM)] * 2,
        out_specs=(VMEM, VMEM),
        scratch_shapes=[pltpu.SemaphoreType.DMA((2, 6))],
        name="parts",
    )(in_hbm(fc1_weight.T), in_hbm(fc2_weight))

    right_p = come_from(own_p, dx=1)
    flip_q = come_from(own_q, dy=-1)
    left_p = come_from(own_p, dx=-1)
    flip_p = come_from(own_p, dy=1)
    over_p = come_from(right_p, dx=1)
    flip_right_p = come_from(right_p, dy=1)
    flip_left_q = come_from(flip_q, dx=-1)

    places = (
        ((0, 0, 0), (0, 0, 1))
        + ((1, 0, 0), (-1, 0, 0), (0, 1, 0), (0, 1, 1))
        + ((1, 0, 1), (-1, 0, 1), (1, 1, 0), (-1, 1, 0), (2, 0, 0), (-1, 1, 1))
        + ((1, 1, 1), (2, 0, 1), (2, 1, 0), (2, 1, 1))
    )
    shards = fc1_bias.shape[0] // hidden_here
    units = len(places) * PART
    bias = kernel_of(functools.partial(bias_kernel, hidden_here, places), 4)(
        out_shape=pltpu.VMEM((-(-units // TILE), TILE), jnp.float32),
        in_specs=[VMEM],
        out_specs=VMEM,
        scratch_shapes=[
            pltpu.VMEM((1, fc1_bias.shape[0]), jnp.float32),
            pltpu.VMEM((4 * shards, TILE), jnp.float32),
        ],
        name="bias",
    )(fc1_bias)

    wide = pltpu.VMEM((tokens, width), jnp.float32)
    hidden = after(hidden, own_p)
    normed = kernel_of(norm_kernel, 4)(
        out_shape=pltpu.VMEM((tokens, width), jnp.bfloat16),
        in_specs=[VMEM] * 3,
        out_specs=VMEM,
        name="norm",
    )(hidden, ln_gain, ln_bias)
    other = come_from(normed, dc=1)
    images = after(image_emb, normed).astype(jnp.float32)
    image_unit = (
        images * lax.rsqrt(jnp.sum(images * images, axis=-1, keepdims=True) + 1e-06)
    ).astype(jnp.bfloat16)
    pictures = [image_unit] + [come_from(image_unit, dz=d) for d in (1, 2, 3)]

    def scratch(first, last):
        return [pltpu.VMEM((last - first, width), jnp.bfloat16)] * 2

    both = pltpu.VMEM((2 * tokens, width), jnp.float32)
    normed, total, keep = kernel_of(functools.partial(first_kernel, TILE))(
        out_shape=(
            pltpu.VMEM((2 * tokens, width), jnp.bfloat16),
            both,
            pltpu.VMEM(text_ids.shape, jnp.float32),
        ),
        in_specs=[VMEM] * 6,
        out_specs=(VMEM,) * 3,
        scratch_shapes=scratch(0, TILE),
        name="units_first",
    )(normed, other, bias, text_ids, own_p, own_q)

    def add_units(first, last, total, parts, name):
        parts = parts[first // PART : -(-last // PART)]
        return kernel_of(functools.partial(add_kernel, first, last, len(parts)))(
            out_shape=both,
            in_specs=[VMEM] * (3 + len(parts)),
            out_specs=VMEM,
            scratch_shapes=scratch(first, last),
            input_output_aliases={2: 0},
            name=name,
        )(normed, bias, total, *parts)

    right_p, left_p, flip_p = after((right_p, left_p, flip_p), total, pictures)
    right_q = come_from(right_p, dz=1)
    left_q = come_from(left_p, dz=-1)
    flip_left_p = come_from(left_p, dy=-1)
    parts = (own_p, own_q, right_p, left_p, flip_p, flip_q)
    total = add_units(TILE, 768, total, parts, "units_second")

    over_p, flip_right_p, flip_left_q = after((over_p, flip_right_p, flip_left_q), total)
    flip_over_q = come_from(flip_left_q, dx=-1)
    flip_right_q = come_from(flip_right_p, dz=1)
    over_q = come_from(over_p, dz=-1)
    flip_over_p = come_from(over_p, dy=1)

    tiles = jnp.transpose(after(teacher_logits, total), (1, 2, 0))
    kinds = [pltpu.VMEM((n, *tiles.shape[1:]), tiles.dtype) for n in (4, 4, 8)]
    tiles_own, tiles_near, tiles_far = kernel_of(tile_kernel, 4)(
        out_shape=tuple(kinds), in_specs=[VMEM], out_specs=(VMEM,) * 3, name="tiles"
    )(tiles)
    tiles_far = come_from(tiles_far, dy=2)

    parts = parts + (right_q, left_q, flip_right_p, flip_left_p, over_p, flip_left_q)
    total = add_units(768, 1536, total, parts, "units_third")

    first, last = 1536, units
    parts = (parts + (flip_right_q, over_q, flip_over_p, flip_over_q))[first // PART :]

    rows = pltpu.VMEM((last - first, width), jnp.bfloat16)
    partial, up, down = kernel_of(
        functools.partial(finish_other_kernel, first, last, len(parts))
    )(
        out_shape=(wide, rows, rows),
        in_specs=[VMEM] * (3 + len(parts)),
        out_specs=(VMEM,) * 3,
        name="finish_other",
    )(normed, bias, total, *parts)
    there_part = come_from(partial, dc=1)
    here_part = kernel_of(functools.partial(finish_own_kernel, first, last))(
        out_shape=wide,
        in_specs=[VMEM] * 7,
        out_specs=VMEM,
        name="finish_own",
    )(normed, bias, total, up, down, hidden, fc2_bias)
    text_unit = kernel_of(unit_kernel, 6)(
        out_shape=pltpu.VMEM((texts_here, width), jnp.bfloat16),
        in_specs=[VMEM] * 7,
        out_specs=VMEM,
        scratch_shapes=[pltpu.VMEM((texts_here, width), jnp.float32)],
        name="unit",
    )(here_part, there_part, final_gain, final_bias, keep, head_weight, head_bias)

    across = come_from(text_unit, dy=2)
    near_x = [text_unit] + [come_from(text_unit, dx=d) for d in NEAR[1:]]
    line = jnp.concatenate(near_x, axis=0)
    across = [across] + [come_from(across, dx=d) for d in NEAR[1:]]
    lines = [line, come_from(line, dy=1), jnp.concatenate(across, axis=0), come_from(line, dy=-1)]
    tiles_near, tiles_far = after((tiles_near, tiles_far), text_unit)
    tiles_swap = kernel_of(pack_kernel, 4)(
        out_shape=pltpu.VMEM(tiles_far.shape, tiles_far.dtype),
        in_specs=[VMEM] * 2,
        out_specs=VMEM,
        name="pack",
    )(tiles_near, tiles_far)
    tile_sets = (tiles_own, tiles_far, come_from(tiles_swap, dc=1))
    lines = lines + [come_from(part, dc=1) for part in lines]
    grads = kernel_of(score_kernel, 6)(
        out_shape=tuple(
            pltpu.VMEM((texts_here, width), kind)
            for kind in (jnp.float32, jnp.bfloat16, jnp.bfloat16, jnp.bfloat16)
        ),
        in_specs=[SMEM] * 2 + [VMEM] * 15,
        out_specs=(VMEM,) * 4,
        scratch_shapes=[
            pltpu.VMEM((4 * texts_here, width), jnp.bfloat16),
            pltpu.VMEM((4, 2, 4 * texts_here, 4 * texts_here), jnp.bfloat16),
        ],
        name="scores",
    )(logit_scale, logit_bias, *lines, *pictures, *tile_sets)
    total = grads[0]
    for d in (1, 2, 3):
        total = total + come_from(grads[d], dz=-d).astype(jnp.float32)
    return logit_scale[0] * total


def solution(mesh):
    placed = (
        P(("dp", "fsdp"), None),
        P(("dp", "fsdp"), None),
        P(),
        P(),
        P(None, "fsdp"),
        P(),
        P("fsdp", None),
        P(),
        P(),
        P(),
        P(),
        P(),
        P(("dp", "fsdp"), None),
        P("dp", None, "fsdp"),
        P(),
        P(),
    )
    return jax.shard_map(
        on_device, mesh=mesh, in_specs=placed, out_specs=P(("dp", "fsdp"), None), check_vma=False
    )
```

```python
import functools

import jax
import jax.numpy as jnp
from jax import lax
from jax.experimental import pallas as pl
from jax.experimental.pallas import tpu as pltpu
from jax.sharding import PartitionSpec as P


AXES = ("dp", "fsdp")
DEVICES = 256
PART = 136
TILE = 256


def place_of(device):
    dp, fs = divmod(device, 8)
    return fs % 4, ((dp >> 1) & 1) * 2 + (fs >> 2), dp >> 2, dp & 1


def device_at(x, y, z, c):
    x, y, z = x % 4, y % 4, z % 8
    return (z * 4 + (y >> 1) * 2 + c) * 8 + (y & 1) * 4 + x


def come_from(array, dx=0, dy=0, dz=0, dc=0):
    pairs = []
    for target in range(DEVICES):
        x, y, z, c = place_of(target)
        pairs.append((device_at(x + dx, y + dy, z + dz, c ^ dc), target))
    return lax.ppermute(array, AXES, pairs)


def here():
    dp, fs = lax.axis_index("dp"), lax.axis_index("fsdp")
    return fs % 4, ((dp // 2) % 2) * 2 + fs // 4, dp // 4, dp % 2


def normalise(values, gain, shift):
    centre = jnp.mean(values, axis=-1, keepdims=True)
    spread = jnp.mean((values - centre) ** 2, axis=-1, keepdims=True)
    return (values - centre) * lax.rsqrt(spread + 1e-06) * gain + shift


BLOCK = 128
ROWS_STEP = 256


def over_blocks(tokens, body):
    def step(i, carry):
        body(pl.ds(pl.multiple_of(i * BLOCK, BLOCK), BLOCK), i)
        return carry

    lax.fori_loop(0, tokens // BLOCK, step, 0)


def norm_kernel(hidden, gain, shift, normed):
    def body(rows, _):
        normed[rows] = normalise(
            hidden[rows].astype(jnp.float32), gain[...].reshape(1, -1), shift[...].reshape(1, -1)
        ).astype(jnp.bfloat16)

    over_blocks(hidden.shape[0], body)


def hidden_units(normed, up, bias):
    pre = (
        lax.dot_general(normed, up, (((1,), (1,)), ((), ())), preferred_element_type=jnp.float32)
        + bias
    )
    return jax.nn.gelu(pre, approximate=True).astype(jnp.bfloat16)


def cut(first, last, more=()):
    cuts = {first, last, *more} | {u for u in range(first, last) if u % PART == 0}
    cuts = sorted(cuts)
    return [(lo // PART, lo % PART, hi - lo, lo - first) for lo, hi in zip(cuts, cuts[1:])]


def assemble(first, last, parts, up, down):
    skipped = first // PART
    for part, row, rows, unit in cut(first, last):
        ref = parts[part - skipped]
        up[pl.ds(unit, rows)] = ref[pl.ds(row, rows)]
        down[pl.ds(unit, rows)] = ref[pl.ds(PART + row, rows)]


def bias_kernel(shard, places, flat, tiles, line, quarters):
    x, y, z, c = here()
    line[...] = flat[...].reshape(1, -1)
    quarters[...] = jnp.zeros(quarters.shape, quarters.dtype)
    for s in range(flat.shape[0] // shard):
        for q in range(4):
            size = min(PART, shard - q * PART)
            quarters[pl.ds(4 * s + q, 1), pl.ds(0, size)] = line[
                :, pl.ds(s * shard + q * PART, size)
            ]
    tiles[...] = jnp.zeros(tiles.shape, tiles.dtype)
    for part, row, rows, unit in cut(0, len(places) * PART, range(0, len(places) * PART, TILE)):
        dx, dy, other = places[part]
        place = (((y + dy) % 2) * 4 + (x + dx + 4) % 4) * 4 + 2 * c + (z + other) % 2
        values = quarters[pl.ds(place, 1), :]
        tiles[pl.ds(unit // TILE, 1), pl.ds(unit % TILE, rows)] = values[:, row : row + rows]


def part_kernel(ups, downs, *refs):
    outs, sems = refs[:2], refs[2]
    _, _, z, c = here()
    size = ups.shape[0]
    full, rest = (size - 3 * PART) // 8 * 8, (size - 3 * PART) % 8

    def whole(k, row):
        return [
            pltpu.make_async_copy(
                weight.at[pl.ds(row, PART)], outs[k].at[pl.ds(side * PART, PART)], sems.at[k, side]
            )
            for side, weight in enumerate((ups, downs))
        ]

    def short(k):
        return [
            pltpu.make_async_copy(
                weight.at[pl.ds(3 * PART + row, count)],
                outs[k].at[pl.ds(side * PART + row, count)],
                sems.at[k, 2 + 2 * side + j],
            )
            for side, weight in enumerate((ups, downs))
            for j, (row, count) in enumerate(((0, full), (full, rest)))
        ]

    for waiting in (False, True):
        for k, out in enumerate(outs):
            quarter = 2 * c + (z + k) % 2

            @pl.when(quarter < 3)
            def _(k=k, quarter=quarter, waiting=waiting):
                for copy in whole(k, pl.multiple_of(quarter * PART, 8)):
                    copy.wait() if waiting else copy.start()

            @pl.when(quarter == 3)
            def _(k=k, out=out, waiting=waiting):
                if not waiting:
                    for side in range(2):
                        zeros = jnp.zeros((PART - full, out.shape[1]), out.dtype)
                        out[pl.ds(side * PART + full, PART - full)] = zeros
                for copy in short(k):
                    copy.wait() if waiting else copy.start()


def add_tiles(first, last, base, normed, bias, before, total, up, down):
    step_rows = min(total.shape[0], ROWS_STEP)

    def step(i, carry):
        start = pl.multiple_of(i * step_rows, step_rows)
        rows = pl.ds(base + start, step_rows)
        here = pl.ds(start, step_rows)
        for unit in range(0, last - first, TILE):
            size = min(TILE, last - first - unit)
            units = pl.ds(unit, size)
            tile_bias = bias[pl.ds((first + unit) // TILE, 1)][:, :size]
            act = hidden_units(normed[rows], up[units], tile_bias)
            term = jnp.dot(act, down[units], preferred_element_type=jnp.float32)
            if unit:
                total[here] += term
            else:
                total[here] = term if before is None else before[rows] + term
        return carry

    lax.fori_loop(0, total.shape[0] // step_rows, step, 0)


def first_kernel(last, own, other, bias, ids, part_p, part_q, normed, total, mask, up, down):
    mask[...] = (ids[...] != 0).astype(jnp.float32)
    count = own.shape[0]
    normed[:count] = own[...]
    normed[count:] = other[...]
    assemble(0, last, (part_p, part_q), up, down)
    add_tiles(0, last, 0, normed, bias, None, total, up, down)


def add_kernel(first, last, count, normed, bias, before, *refs):
    parts, (total, up, down) = refs[:count], refs[count:]
    assemble(first, last, parts, up, down)
    add_tiles(first, last, 0, normed, bias, before, total, up, down)


def finish_other_kernel(first, last, count, normed, bias, before, *refs):
    parts, (total, up, down) = refs[:count], refs[count:]
    assemble(first, last, parts, up, down)
    add_tiles(first, last, total.shape[0], normed, bias, before, total, up, down)


def finish_own_kernel(first, last, normed, bias, before, up, down, hidden, fc2_bias, total):
    def body(rows, _):
        total[rows] = before[rows] + hidden[rows].astype(jnp.float32) + fc2_bias[...].reshape(1, -1)

    over_blocks(total.shape[0], body)
    add_tiles(first, last, 0, normed, bias, total, total, up, down)


def unit_kernel(here_part, there_part, gain, shift, mask, head, head_bias, unit, pooled):
    width = unit.shape[1]
    seq = here_part.shape[0] // unit.shape[0]
    texts = BLOCK // seq

    def body(rows, i):
        out = here_part[rows] + there_part[rows]
        final = normalise(out, gain[...].reshape(1, -1), shift[...].reshape(1, -1))
        block = pl.ds(pl.multiple_of(i * texts, texts), texts)
        keep = mask[block]
        spread = jnp.broadcast_to(keep[:, None, :], (texts, seq, seq)).reshape(texts * seq, seq)
        at_row = lax.broadcasted_iota(jnp.int32, spread.shape, 0) % seq
        at_lane = lax.broadcasted_iota(jnp.int32, spread.shape, 1)
        kept = jnp.sum(jnp.where(at_row == at_lane, spread, 0.0), axis=1, keepdims=True)
        summed = jnp.sum((final * kept).reshape(texts, seq, width), axis=1)
        pooled[block] = summed / jnp.sum(keep, axis=1, keepdims=True)

    over_blocks(here_part.shape[0], body)
    emb = jnp.dot(
        pooled[...].astype(jnp.bfloat16), head[...], preferred_element_type=jnp.float32
    ) + head_bias[...].reshape(1, -1)
    unit[...] = (emb * lax.rsqrt(jnp.sum(emb * emb, axis=-1, keepdims=True) + 1e-06)).astype(
        jnp.bfloat16
    )


NEAR = (0, 1, 2, -1)
ROWS = tuple((dy, dc) for dc in (0, 1) for dy in NEAR)
TILES = ((0, 0), (2, 0), (1, 0), (2, 4))


def tile_kernel(tiles, own, near, far):
    x, y, _, c = here()
    column = (y // 2) * 2 + c
    _, group = tiles.shape[1:]
    half = group // 2
    for m, (target, at) in enumerate(((own, 0), (near, 0), (far, 0), (far, 4))):
        other = (column // 2 + m // 2) % 2 * 2 + (column % 2 + m % 2) % 2
        for d in range(4):
            step = jnp.clip(4 * d + other - column, 0, tiles.shape[0] - 1)
            tile = tiles[step].astype(jnp.float32)
            parts = [
                pltpu.roll(tile[:, k * half : (k + 1) * half], (4 - x) % 4 * (half // 4), 1)
                for k in range(2)
            ]
            target[at + d] = jnp.concatenate(parts, axis=1).astype(tiles.dtype)


def pack_kernel(near, far, both):
    both[:4] = near[...]
    both[4:] = far[4:]


def score_kernel(logit_scale, logit_bias, *refs):
    lines, images, tiles = refs[:8], refs[8:12], refs[12:15]
    grads, pictures, targets = refs[15:19], refs[19], refs[20]
    _, y, _, c = here()
    column = (y // 2) * 2 + c
    size, width = images[0].shape
    count = lines[0].shape[0]
    for d in range(4):
        pictures[pl.ds(d * size, size)] = images[d][...]
    for m in range(4):
        source, at = TILES[m]
        tile = tiles[source][at : at + 4].reshape(4 * size, 2 * count)
        for k in range(2):
            targets[m, k] = tile[:, k * count : (k + 1) * count]
    scale, offset = logit_scale[0], logit_bias[0]
    pics = pictures[...]
    total = jnp.zeros((4 * size, width), jnp.float32)
    far = lax.broadcasted_iota(jnp.int32, (4 * size, count), 0) // size
    for r, (dy, dc) in enumerate(ROWS):
        there = (y + dy + 4) % 4
        block = (there // 2) * 2 + (c + dc) % 2
        m = (there // 2 + y // 2) % 2 * 2 + dc
        units = lines[r][...]
        score = (
            scale
            * lax.dot_general(
                pics, units, (((1,), (1,)), ((), ())), preferred_element_type=jnp.float32
            )
            + offset
        )
        target = targets[m, there % 2].astype(jnp.float32)
        step = 4 * far + (column - block)
        weight = jnp.where(
            (step >= 0) & (step < 12), jax.nn.sigmoid(score) - jax.nn.sigmoid(target), 0.0
        ).astype(jnp.bfloat16)
        total = total + jnp.dot(weight, units, preferred_element_type=jnp.float32)
    for d in range(4):
        grads[d][...] = total[d * size : (d + 1) * size].astype(grads[d].dtype)


VMEM = pl.BlockSpec(memory_space=pltpu.VMEM)
ANY = pl.BlockSpec(memory_space=pl.ANY)
SMEM = pl.BlockSpec(memory_space=pltpu.SMEM)


def kernel_of(body, mib=10):
    return functools.partial(
        pl.pallas_call, body, compiler_params=pltpu.CompilerParams(vmem_limit_bytes=mib << 20)
    )


def in_hbm(array):
    return pltpu.with_memory_space_constraint(array, pltpu.HBM)


def after(values, *others):
    return lax.optimization_barrier((values, others))[0]


def on_device(
    hidden,
    text_ids,
    ln_gain,
    ln_bias,
    fc1_weight,
    fc1_bias,
    fc2_weight,
    fc2_bias,
    final_gain,
    final_bias,
    head_weight,
    head_bias,
    image_emb,
    teacher_logits,
    logit_scale,
    logit_bias,
):
    tokens, width = hidden.shape
    texts_here, _ = text_ids.shape
    hidden_here = fc1_weight.shape[1]

    part = pltpu.VMEM((2 * PART, width), jnp.bfloat16)
    own_p, own_q = kernel_of(part_kernel, 4)(
        out_shape=(part, part),
        in_specs=[pl.BlockSpec(memory_space=pltpu.HBM)] * 2,
        out_specs=(VMEM, VMEM),
        scratch_shapes=[pltpu.SemaphoreType.DMA((2, 6))],
        name="parts",
    )(in_hbm(fc1_weight.T), in_hbm(fc2_weight))

    right_p = come_from(own_p, dx=1)
    flip_q = come_from(own_q, dy=-1)
    left_p = come_from(own_p, dx=-1)
    flip_p = come_from(own_p, dy=1)
    over_p = come_from(right_p, dx=1)
    flip_right_p = come_from(right_p, dy=1)
    flip_left_q = come_from(flip_q, dx=-1)

    places = (
        ((0, 0, 0), (0, 0, 1))
        + ((1, 0, 0), (-1, 0, 0), (0, 1, 0), (0, 1, 1))
        + ((1, 0, 1), (-1, 0, 1), (1, 1, 0), (-1, 1, 0), (2, 0, 0), (-1, 1, 1))
        + ((1, 1, 1), (2, 0, 1), (2, 1, 0), (2, 1, 1))
    )
    shards = fc1_bias.shape[0] // hidden_here
    units = len(places) * PART
    bias = kernel_of(functools.partial(bias_kernel, hidden_here, places), 4)(
        out_shape=pltpu.VMEM((-(-units // TILE), TILE), jnp.float32),
        in_specs=[VMEM],
        out_specs=VMEM,
        scratch_shapes=[
            pltpu.VMEM((1, fc1_bias.shape[0]), jnp.float32),
            pltpu.VMEM((4 * shards, TILE), jnp.float32),
        ],
        name="bias",
    )(fc1_bias)

    wide = pltpu.VMEM((tokens, width), jnp.float32)
    hidden = after(hidden, own_p)
    normed = kernel_of(norm_kernel, 4)(
        out_shape=pltpu.VMEM((tokens, width), jnp.bfloat16),
        in_specs=[VMEM] * 3,
        out_specs=VMEM,
        name="norm",
    )(hidden, ln_gain, ln_bias)
    other = come_from(normed, dc=1)
    images = after(image_emb, normed).astype(jnp.float32)
    image_unit = (
        images * lax.rsqrt(jnp.sum(images * images, axis=-1, keepdims=True) + 1e-06)
    ).astype(jnp.bfloat16)
    pictures = [image_unit] + [come_from(image_unit, dz=d) for d in (1, 2, 3)]

    tiles = jnp.transpose(after(teacher_logits, normed), (1, 2, 0))
    kinds = [pltpu.VMEM((n, *tiles.shape[1:]), tiles.dtype) for n in (4, 4, 8)]
    tiles_own, tiles_near, tiles_far = kernel_of(tile_kernel, 4)(
        out_shape=tuple(kinds), in_specs=[VMEM], out_specs=(VMEM,) * 3, name="tiles"
    )(tiles)
    tiles_far = come_from(tiles_far, dy=2)

    def scratch(first, last):
        return [pltpu.VMEM((last - first, width), jnp.bfloat16)] * 2

    both = pltpu.VMEM((2 * tokens, width), jnp.float32)
    normed, total, keep = kernel_of(functools.partial(first_kernel, TILE))(
        out_shape=(
            pltpu.VMEM((2 * tokens, width), jnp.bfloat16),
            both,
            pltpu.VMEM(text_ids.shape, jnp.float32),
        ),
        in_specs=[VMEM] * 6,
        out_specs=(VMEM,) * 3,
        scratch_shapes=scratch(0, TILE),
        name="units_first",
    )(normed, other, bias, text_ids, own_p, own_q)

    def add_units(first, last, total, parts, name):
        parts = parts[first // PART : -(-last // PART)]
        return kernel_of(functools.partial(add_kernel, first, last, len(parts)))(
            out_shape=both,
            in_specs=[VMEM] * (3 + len(parts)),
            out_specs=VMEM,
            scratch_shapes=scratch(first, last),
            input_output_aliases={2: 0},
            name=name,
        )(normed, bias, total, *parts)

    right_p, left_p, flip_p = after((right_p, left_p, flip_p), total, pictures)
    right_q = come_from(right_p, dz=1)
    left_q = come_from(left_p, dz=-1)
    flip_left_p = come_from(left_p, dy=-1)
    parts = (own_p, own_q, right_p, left_p, flip_p, flip_q)
    total = add_units(TILE, 2 * TILE, total, parts, "units_second")

    over_p, flip_right_p, flip_left_q = after((over_p, flip_right_p, flip_left_q), total)
    flip_over_q = come_from(flip_left_q, dx=-1)
    flip_right_q = come_from(flip_right_p, dz=1)
    over_q = come_from(over_p, dz=-1)
    flip_over_p = come_from(over_p, dy=1)

    parts = parts + (right_q, left_q, flip_right_p, flip_left_p, over_p, flip_left_q)
    total = add_units(2 * TILE, 1536, total, parts, "units_third")

    first, last = 1536, units
    parts = (parts + (flip_right_q, over_q, flip_over_p, flip_over_q))[first // PART :]

    rows = pltpu.VMEM((last - first, width), jnp.bfloat16)
    partial, up, down = kernel_of(
        functools.partial(finish_other_kernel, first, last, len(parts))
    )(
        out_shape=(wide, rows, rows),
        in_specs=[VMEM] * (3 + len(parts)),
        out_specs=(VMEM,) * 3,
        name="finish_other",
    )(normed, bias, total, *parts)
    there_part = come_from(partial, dc=1)
    here_part = kernel_of(functools.partial(finish_own_kernel, first, last))(
        out_shape=wide,
        in_specs=[VMEM] * 7,
        out_specs=VMEM,
        name="finish_own",
    )(normed, bias, total, up, down, hidden, fc2_bias)
    text_unit = kernel_of(unit_kernel, 6)(
        out_shape=pltpu.VMEM((texts_here, width), jnp.bfloat16),
        in_specs=[VMEM] * 7,
        out_specs=VMEM,
        scratch_shapes=[pltpu.VMEM((texts_here, width), jnp.float32)],
        name="unit",
    )(here_part, there_part, final_gain, final_bias, keep, head_weight, head_bias)

    across = come_from(text_unit, dy=2)
    near_x = [text_unit] + [come_from(text_unit, dx=d) for d in NEAR[1:]]
    line = jnp.concatenate(near_x, axis=0)
    across = [across] + [come_from(across, dx=d) for d in NEAR[1:]]
    lines = [line, come_from(line, dy=1), jnp.concatenate(across, axis=0), come_from(line, dy=-1)]
    tiles_near, tiles_far = after((tiles_near, tiles_far), text_unit)
    tiles_swap = kernel_of(pack_kernel, 4)(
        out_shape=pltpu.VMEM(tiles_far.shape, tiles_far.dtype),
        in_specs=[VMEM] * 2,
        out_specs=VMEM,
        name="pack",
    )(tiles_near, tiles_far)
    tile_sets = (tiles_own, tiles_far, come_from(tiles_swap, dc=1))
    lines = lines + [come_from(part, dc=1) for part in lines]
    grads = kernel_of(score_kernel, 6)(
        out_shape=tuple(
            pltpu.VMEM((texts_here, width), kind)
            for kind in (jnp.float32, jnp.bfloat16, jnp.bfloat16, jnp.bfloat16)
        ),
        in_specs=[SMEM] * 2 + [VMEM] * 15,
        out_specs=(VMEM,) * 4,
        scratch_shapes=[
            pltpu.VMEM((4 * texts_here, width), jnp.bfloat16),
            pltpu.VMEM((4, 2, 4 * texts_here, 4 * texts_here), jnp.bfloat16),
        ],
        name="scores",
    )(logit_scale, logit_bias, *lines, *pictures, *tile_sets)
    total = grads[0]
    for d in (1, 2, 3):
        total = total + come_from(grads[d], dz=-d).astype(jnp.float32)
    return logit_scale[0] * total


def solution(mesh):
    placed = (
        P(("dp", "fsdp"), None),
        P(("dp", "fsdp"), None),
        P(),
        P(),
        P(None, "fsdp"),
        P(),
        P("fsdp", None),
        P(),
        P(),
        P(),
        P(),
        P(),
        P(("dp", "fsdp"), None),
        P("dp", None, "fsdp"),
        P(),
        P(),
    )
    return jax.shard_map(
        on_device, mesh=mesh, in_specs=placed, out_specs=P(("dp", "fsdp"), None), check_vma=False
    )
```
